128 devices in a mesh: ctx: 32 (over y, z_lo, x), ep: 4 (over z_hi, core).
Axes of the slice: x: 4, y: 4, z: 4 (z_hi: 2, z_lo: 2; z = z_hi * 2 + z_lo), core: 2. Of those that a mesh axis runs over, the one named last changes fastest.
Arguments:
- block_input_rows: bfloat16 [16384, 4096], P(('ctx', 'ep')), may hold values from -6 to 6
- output_gradient: bfloat16 [16384, 4096], P(('ctx', 'ep')), may hold values from -12 to 12
- expert_choice_index: int32 [16384, 8], P(('ctx', 'ep')), may hold values from 0 to 127, all different within a row; in each aligned block of 128 rows (0 to 127, 128 to 255, ...) at most 9 rows name the same one
- routing_weight_rows: float32 [16384, 8], P(('ctx', 'ep')), may hold values from 0.03 to 0.5
- frozen_gate_weight: bfloat16 [128, 4096, 768], P(('ctx', 'ep')), may hold values from -0.09375 to 0.09375
- frozen_up_weight: bfloat16 [128, 4096, 768], P(('ctx', 'ep')), may hold values from -0.09375 to 0.09375
- frozen_down_weight: bfloat16 [128, 768, 4096], P(('ctx', 'ep')), may hold values from -0.21875 to 0.21875
- gate_adapter_inmap: bfloat16 [128, 16, 4096], P(('ctx', 'ep')), may hold values from -0.09375 to 0.09375
- gate_adapter_outmap: bfloat16 [128, 16, 768], P(('ctx', 'ep')), may hold values from -0.21875 to 0.21875
- up_adapter_inmap: bfloat16 [128, 16, 4096], P(('ctx', 'ep')), may hold values from -0.09375 to 0.09375
- up_adapter_outmap: bfloat16 [128, 16, 768], P(('ctx', 'ep')), may hold values from -0.21875 to 0.21875
- down_adapter_inmap: bfloat16 [128, 16, 768], P(('ctx', 'ep')), may hold values from -0.21875 to 0.21875
- down_adapter_outmap: bfloat16 [128, 16, 4096], P(('ctx', 'ep')), may hold values from -0.09375 to 0.09375
- stored_gate_preact: bfloat16 [128, 1152, 768], P(('ctx', 'ep')), may hold values from -8 to 8
- stored_up_preact: bfloat16 [128, 1152, 768], P(('ctx', 'ep')), may hold values from -6 to 6
Outputs:
- grad_in: bfloat16 [16384, 4096], P(('ctx', 'ep'))
- gate_input_gradient: bfloat16 [128, 16, 4096], P(('ctx', 'ep'))
- gate_output_gradient: bfloat16 [128, 16, 768], P(('ctx', 'ep'))
- up_input_gradient: bfloat16 [128, 16, 4096], P(('ctx', 'ep'))
- up_output_gradient: bfloat16 [128, 16, 768], P(('ctx', 'ep'))
- down_input_gradient: bfloat16 [128, 16, 768], P(('ctx', 'ep'))
- down_output_gradient: bfloat16 [128, 16, 4096], P(('ctx', 'ep'))
The draws below stay inside these ranges and needn't reach their ends.
Inputs may be any that keep to these rules, and one draw needn't show every extreme that they name: `expert_choice_index`: A token names 8 different experts. Among the tokens of one device, an expert is named by at most 9 of them, and in every draw some expert by exactly 9.
All inputs are finite; a program needn't handle non-finite values.
Results may differ from the reference program's by a relative error of at most 0.0065.
Values may be sent and summed in bfloat16 or wider, within the bound.
A program may use at most 256 MiB of HBM per device.

```python
import math
import jax
import jax.numpy as jnp
import numpy as np
from jax import lax

HIDDEN_WIDTH = 4096
HALF_HIDDEN = 768
ADAPTER_RANK = 16
TOPK = 8
TOK_DEV = 128
EXPERT_COUNT = 128
TOKENS = 16384
CAP = 9
SLOTS = 1152


def block_levels(stream_key, shape, cuts, low, top_value):
    factor_of, own = 1.0, jax.random.fold_in(stream_key, 6)
    for position, blocks in cuts:
        heights = jnp.exp(jax.random.uniform(jax.random.fold_in(own, position), (blocks,), jnp.float32, low / len(cuts), top_value / len(cuts)))
        factor_of = factor_of * jnp.repeat(heights, shape[position] // blocks).reshape([-1 if axis == position else 1 for axis in range(len(shape))])
    return factor_of


def deal_out(rng, own, number, rows, number_of, top, limit, skew):
    ranking = jax.random.permutation(rng, number_of)
    packed, usual = portions_of(number_of, rows * top, limit, skew, True), portions_of(number_of, rows * top, limit, skew, False)
    places = jnp.arange(number_of)

    def named(tallies, offset_by):
        used = int((tallies > 0).sum())
        fixed = max(1, used // 4)
        moved = fixed + (places - fixed + offset_by * (used - fixed)) % max(1, number_of - fixed)
        return jnp.zeros((number_of,), jnp.int32).at[ranking[jnp.where(places < fixed, places, moved)]].set(jnp.asarray(tallies, jnp.int32))

    tallies = jnp.where(number % 4 == 0, named(packed, number // 4), named(usual, number - number // 4 - 1))
    mixed = jax.random.permutation(jax.random.fold_in(own, 3), number_of)
    donor, taker = mixed[0:number_of // 2 * 2:2], mixed[1:number_of // 2 * 2:2]
    room = jnp.minimum(tallies[donor] - 1, limit - tallies[taker]) // 2
    room = jnp.where((donor == ranking[0]) | (taker == ranking[0]) | (tallies[taker] == 0), 0, jnp.maximum(room, 0))
    moved = jax.random.randint(jax.random.fold_in(own, 4), (number_of // 2,), 0, 1 << 20) % (room + 1)
    tallies = tallies.at[donor].add(-moved).at[taker].add(moved)
    items = jnp.searchsorted(jnp.cumsum(tallies), jnp.arange(rows * top), side="right").astype(jnp.int32)
    table = items.reshape(top, rows).T
    table = table[jax.random.permutation(jax.random.fold_in(own, 1), rows)]
    offset_by = jax.random.randint(jax.random.fold_in(own, 2), (rows, 1), 0, top)
    return jnp.take_along_axis(table, (jnp.arange(top)[None, :] + offset_by) % top, axis=1)


def portions_of(number_of, total, reach, lean, full):
    portions = [(1 << 20) // math.isqrt(rank ** lean) + 1 for rank in range(1, number_of + 1)]
    largest = reach if full else min(reach, max(-(-total // number_of), total * portions[0] // sum(portions)))
    least = 1 if total - largest >= number_of - 1 else 0
    given, rest = [largest] + [least] * (number_of - 1), total - largest - least * (number_of - 1)
    while rest > 0:
        candidates = [i for i in range(1, number_of) if given[i] < largest] or [i for i in range(1, number_of) if given[i] < reach]
        whole, left = sum([portions[i] for i in candidates]), rest
        for i in candidates:
            addition = min(reach - given[i], max(1, left * portions[i] // whole), rest)
            given[i] = given[i] + addition
            rest = rest - addition
    return np.array(given)


def gaussian(key, shape, width, bound, split=(), held_as=jnp.bfloat16):
    array = width * jax.random.normal(key, shape, jnp.float32)
    if split:
        array = array * block_levels(key, shape, split, -0.22, 0.18)
    return jnp.clip(array, -bound, bound).astype(held_as)


def setup_inputs(seed: int = 0) -> dict:
    key_of = jax.random.split(jax.random.key(seed), 16)
    block_input_rows = gaussian(key_of[0], (TOKENS, HIDDEN_WIDTH), 1.0, 6.0, ((0, 128),))
    output_gradient = gaussian(key_of[1], (TOKENS, HIDDEN_WIDTH), 2.0, 12.0, ((0, 128),))
    expert_choice_index_keys = jax.random.split(jax.random.fold_in(key_of[2], 1), TOKENS // TOK_DEV)
    expert_choice_index_turns = jax.random.permutation(jax.random.fold_in(key_of[2], 3), TOKENS // TOK_DEV)
    expert_choice_index = jax.vmap(lambda own, number: deal_out(jax.random.fold_in(key_of[2], 2), own, number, TOK_DEV, EXPERT_COUNT, TOPK, CAP, 2))(expert_choice_index_keys, expert_choice_index_turns).reshape((TOKENS, TOPK))
    routing_weight_rows = jnp.clip(jnp.exp(math.log(0.5) - 2.8134107 * jax.random.uniform(key_of[3], (TOKENS, TOPK), jnp.float32) ** block_levels(key_of[3], (TOKENS, TOPK), ((0, 128),), -0.2, 0.2)), 0.03, 0.5)
    frozen_gate_weight = gaussian(key_of[4], (EXPERT_COUNT, HIDDEN_WIDTH, HALF_HIDDEN), HIDDEN_WIDTH ** -0.5, 0.09375, ((0, 128),))
    frozen_up_weight = gaussian(key_of[5], (EXPERT_COUNT, HIDDEN_WIDTH, HALF_HIDDEN), HIDDEN_WIDTH ** -0.5, 0.09375, ((0, 128),))
    frozen_down_weight = gaussian(key_of[6], (EXPERT_COUNT, HALF_HIDDEN, HIDDEN_WIDTH), HALF_HIDDEN ** -0.5, 0.21875, ((0, 128),))
    gate_adapter_inmap = gaussian(key_of[7], (EXPERT_COUNT, ADAPTER_RANK, HIDDEN_WIDTH), HIDDEN_WIDTH ** -0.5, 0.09375, ((0, 128),))
    gate_adapter_outmap = gaussian(key_of[8], (EXPERT_COUNT, ADAPTER_RANK, HALF_HIDDEN), HALF_HIDDEN ** -0.5, 0.21875, ((0, 128),))
    up_adapter_inmap = gaussian(key_of[9], (EXPERT_COUNT, ADAPTER_RANK, HIDDEN_WIDTH), HIDDEN_WIDTH ** -0.5, 0.09375, ((0, 128),))
    up_adapter_outmap = gaussian(key_of[10], (EXPERT_COUNT, ADAPTER_RANK, HALF_HIDDEN), HALF_HIDDEN ** -0.5, 0.21875, ((0, 128),))
    down_adapter_inmap = gaussian(key_of[11], (EXPERT_COUNT, ADAPTER_RANK, HALF_HIDDEN), HALF_HIDDEN ** -0.5, 0.21875, ((0, 128),))
    down_adapter_outmap = gaussian(key_of[12], (EXPERT_COUNT, ADAPTER_RANK, HIDDEN_WIDTH), HIDDEN_WIDTH ** -0.5, 0.09375, ((0, 128),))
    stored_gate_preact = gaussian(key_of[13], (EXPERT_COUNT, SLOTS, HALF_HIDDEN), 1.5, 8.0, ((0, 128),))
    stored_up_preact = gaussian(key_of[14], (EXPERT_COUNT, SLOTS, HALF_HIDDEN), 1.0, 6.0, ((0, 128),))
    return dict(block_input_rows=block_input_rows, output_gradient=output_gradient, expert_choice_index=expert_choice_index, routing_weight_rows=routing_weight_rows, frozen_gate_weight=frozen_gate_weight, frozen_up_weight=frozen_up_weight, frozen_down_weight=frozen_down_weight, gate_adapter_inmap=gate_adapter_inmap, gate_adapter_outmap=gate_adapter_outmap, up_adapter_inmap=up_adapter_inmap, up_adapter_outmap=up_adapter_outmap, down_adapter_inmap=down_adapter_inmap, down_adapter_outmap=down_adapter_outmap, stored_gate_preact=stored_gate_preact, stored_up_preact=stored_up_preact)


adapter_scale = 2.0


def contract_matrices(left_mat, right_mat, left_axis, right_axis):
    return lax.dot_general(left_mat, right_mat, (((left_axis,), (right_axis,)), ((), ())), preferred_element_type=jnp.float32)


def expert_backward(gathered_input_rows, gathered_gradient_rows, gate_pre, up_pre, frozen_gate_weight, frozen_up_weight, frozen_down_weight, gate_adapter_input, gate_out, up_adapter_input, up_out, down_adapter_input, down_adapter_output):
    gate_value = gate_pre.astype(jnp.float32)
    up_value = up_pre.astype(jnp.float32)
    sigmoid_gate = jax.nn.sigmoid(gate_value)
    silu_gate = gate_value * sigmoid_gate
    hidden_activation = (silu_gate * up_value).astype(jnp.bfloat16)
    down_adapter_delta = contract_matrices(hidden_activation, down_adapter_input, 1, 1).astype(jnp.bfloat16)
    adapter_gradient = contract_matrices(gathered_gradient_rows, down_adapter_output, 1, 1).astype(jnp.bfloat16)
    down_output_gradient = adapter_scale * contract_matrices(down_adapter_delta, gathered_gradient_rows, 0, 0)
    down_input_gradient = adapter_scale * contract_matrices(adapter_gradient, hidden_activation, 0, 0)
    hidden_gradient_rows = contract_matrices(gathered_gradient_rows, frozen_down_weight, 1, 1) + adapter_scale * contract_matrices(adapter_gradient, down_adapter_input, 1, 0)
    gate_gradient_rows = (hidden_gradient_rows * up_value * sigmoid_gate * (1.0 + gate_value * (1.0 - sigmoid_gate))).astype(jnp.bfloat16)
    up_gradient_rows = (hidden_gradient_rows * silu_gate).astype(jnp.bfloat16)
    gate_adapter_delta = contract_matrices(gathered_input_rows, gate_adapter_input, 1, 1).astype(jnp.bfloat16)
    up_adapter_delta = contract_matrices(gathered_input_rows, up_adapter_input, 1, 1).astype(jnp.bfloat16)
    gate_output_gradient = adapter_scale * contract_matrices(gate_adapter_delta, gate_gradient_rows, 0, 0)
    up_output_gradient = adapter_scale * contract_matrices(up_adapter_delta, up_gradient_rows, 0, 0)
    gate_backward_rows = contract_matrices(gate_gradient_rows, gate_out, 1, 1).astype(jnp.bfloat16)
    up_backward_rows = contract_matrices(up_gradient_rows, up_out, 1, 1).astype(jnp.bfloat16)
    gate_input_gradient = adapter_scale * contract_matrices(gate_backward_rows, gathered_input_rows, 0, 0)
    up_input_gradient = adapter_scale * contract_matrices(up_backward_rows, gathered_input_rows, 0, 0)
    scattered_output_rows = contract_matrices(gate_gradient_rows, frozen_gate_weight, 1, 1) + contract_matrices(up_gradient_rows, frozen_up_weight, 1, 1)
    scattered_output_rows = scattered_output_rows + adapter_scale * (contract_matrices(gate_backward_rows, gate_adapter_input, 1, 0) + contract_matrices(up_backward_rows, up_adapter_input, 1, 0))
    expert_outcomes = (gate_input_gradient.astype(jnp.bfloat16), gate_output_gradient.astype(jnp.bfloat16), up_input_gradient.astype(jnp.bfloat16), up_output_gradient.astype(jnp.bfloat16), down_input_gradient.astype(jnp.bfloat16), down_output_gradient.astype(jnp.bfloat16))
    return scattered_output_rows.astype(jnp.bfloat16), expert_outcomes


def reference(block_input_rows, output_gradient, expert_choice_index, routing_weight_rows, frozen_gate_weight, frozen_up_weight, frozen_down_weight, gate_adapter_inmap, gate_adapter_outmap, up_adapter_inmap, up_adapter_outmap, down_adapter_inmap, down_adapter_outmap, stored_gate_preact, stored_up_preact):
    blocks = TOKENS // TOK_DEV
    pick_count = TOK_DEV * TOPK
    block_ids = expert_choice_index.reshape(blocks, pick_count)
    onehot = (block_ids[:, :, None] == jnp.arange(EXPERT_COUNT, dtype=jnp.int32)[None, None, :]).astype(jnp.int32)
    running = jnp.cumsum(onehot, axis=1, dtype=jnp.int32)
    slot_num = jnp.sum(onehot * running, axis=2).astype(jnp.int32) - 1
    slot_global = (jnp.arange(blocks, dtype=jnp.int32)[:, None] * CAP + slot_num).reshape(-1).astype(jnp.int32)
    flat_ids = expert_choice_index.reshape(-1).astype(jnp.int32)
    token_pick = (jnp.arange(TOKENS * TOPK, dtype=jnp.int32) // TOPK).astype(jnp.int32)
    token_index_table = jnp.full((EXPERT_COUNT, SLOTS), TOKENS, jnp.int32).at[flat_ids, slot_global].set(token_pick)
    routing_weight_table = jnp.zeros((EXPERT_COUNT, SLOTS), routing_weight_rows.dtype).at[flat_ids, slot_global].set(routing_weight_rows.reshape(-1))

    def single_expert_backward(carried, entries):
        (tokens_here, weights_here, gate_w, up_w, down_w, gate_adapter_input, gate_out, up_adapter_input, up_out, down_adapter_input, down_adapter_output, gate_pre, up_pre) = entries
        filled = tokens_here < TOKENS
        safe_index = jnp.minimum(tokens_here, TOKENS - 1)
        gathered_input_rows = jnp.where(filled[:, None], block_input_rows[safe_index], jnp.zeros((), block_input_rows.dtype))
        gathered_gradient_rows = (weights_here[:, None] * output_gradient[safe_index].astype(jnp.float32)).astype(jnp.bfloat16)
        scattered_output_rows, expert_outcomes = expert_backward(gathered_input_rows, gathered_gradient_rows, gate_pre, up_pre, gate_w, up_w, down_w, gate_adapter_input, gate_out, up_adapter_input, up_out, down_adapter_input, down_adapter_output)
        carried = carried.at[tokens_here].add(scattered_output_rows.astype(jnp.float32))
        return carried, expert_outcomes

    initial_sum_state = jnp.zeros((TOKENS + 1, HIDDEN_WIDTH), jnp.float32)
    reduced_total, expert_outcomes = lax.scan(single_expert_backward, initial_sum_state, (token_index_table, routing_weight_table, frozen_gate_weight, frozen_up_weight, frozen_down_weight, gate_adapter_inmap, gate_adapter_outmap, up_adapter_inmap, up_adapter_outmap, down_adapter_inmap, down_adapter_outmap, stored_gate_preact, stored_up_preact))
    grad_in = reduced_total[:TOKENS].astype(jnp.bfloat16)
    return grad_in, expert_outcomes[0], expert_outcomes[1], expert_outcomes[2], expert_outcomes[3], expert_outcomes[4], expert_outcomes[5]
```

```python
import functools

import jax
import jax.numpy as jnp
from jax import lax
from jax.experimental import pallas as pl
from jax.experimental.pallas import tpu as pltpu
from jax.sharding import PartitionSpec as P

MESH = pl.DeviceIdType.MESH
ROLES = ((0, 1, 2), (1, 2, 0), (2, 0, 1))
WID = (1280, 1280, 1536)
OFF = (0, 1280, 2560)
CHUNK = 256
F32 = jnp.float32
BF16 = jnp.bfloat16
adapter_scale = 2.0


def coords():
    c = lax.axis_index("ctx")
    e = lax.axis_index("ep")
    x = lax.rem(c, 4)
    y = c // 8
    z = (e // 2) * 2 + lax.rem(c // 4, 2)
    return (x, y, z), lax.rem(e, 2)


def device(pos, core):
    x, y, z = pos
    return ((y * 2 + lax.rem(z, 2)) * 4 + x, (z // 2) * 2 + core)


def moved(pos, axis, d):
    out = list(pos)
    out[axis] = lax.rem(pos[axis] + d, 4)
    return tuple(out)


def greet(pos, core):
    barrier = pltpu.get_barrier_semaphore()
    other = 1 - core
    peers = [device(pos, other)]
    for axis in range(3):
        for d in (1, 2, 3):
            peers.append(device(moved(pos, axis, d), core))
            peers.append(device(moved(pos, axis, d), other))
    for peer in peers:
        pl.semaphore_signal(barrier, inc=1, device_id=peer, device_id_type=MESH)
    return barrier, len(peers)


def remote(src, dst, ssem, rsem, dev):
    return pltpu.make_async_remote_copy(
        src_ref=src, dst_ref=dst, send_sem=ssem, recv_sem=rsem, device_id=dev, device_id_type=MESH
    )


def expert_ids(j, shape):
    i = lax.broadcasted_iota(jnp.int32, shape, 0)
    v = [None] * 3
    a, b, c = ROLES[j]
    v[a] = i // 32
    v[b] = (i // 8) % 4
    v[c] = (i // 2) % 4
    k = i % 2
    x, y, z = v
    return ((y * 2 + z % 2) * 4 + x) * 4 + (z // 2) * 2 + k


def main_at(ref, j, b, c, k):
    ra, rb, rc = ROLES[j]
    idx = [None] * 3
    idx[ra] = slice(None)
    idx[rb] = b
    idx[rc] = c
    return ref.at[idx[0], idx[1], idx[2], k, :, pl.ds(OFF[j], WID[j])]


def cols(j):
    return [(s, CHUNK) for s in range(0, WID[j], CHUNK)]


def dispatch_kernel(*refs):
    ids_ref, wt_ref, g_ref, x_ref = refs[:4]
    outs = refs[4:13]
    gmain, xmain = outs[0], outs[1]
    tails = (outs[2:5], outs[5:8])
    masks = outs[8]
    scratch = refs[13:]
    ag = scratch[0:3]
    send2 = scratch[3:6]
    recv2 = scratch[6:9]
    send2t = scratch[9:12]
    recv2t = scratch[12:15]
    tab, tabr, pm, wmain, wtail = scratch[15:20]
    sems = scratch[20]
    mains = (gmain, xmain)
    data = (g_ref, x_ref)
    pos, core = coords()
    other = 1 - core
    barrier, count = greet(pos, core)

    row = lax.broadcasted_iota(jnp.int32, (128, 128), 0)
    lane = lax.broadcasted_iota(jnp.int32, (128, 128), 1)
    strict = (row < lane).astype(BF16)
    for j in range(3):
        eid = expert_ids(j, (128, 128))
        hit = jnp.zeros((128, 128), F32)
        wgt = jnp.zeros((128, 128), F32)
        for k in range(8):
            same = eid == ids_ref[k : k + 1, :]
            hit = hit + jnp.where(same, 1.0, 0.0)
            wgt = wgt + jnp.where(same, wt_ref[k : k + 1, :], 0.0)
        rank = jnp.dot(hit.astype(BF16), strict, preferred_element_type=F32)
        code = jnp.where(hit > 0.5, rank, -1.0)
        tab[j, :, 0] = code.reshape(4, 32, 128)
        tab[j, :, 1] = wgt.reshape(4, 32, 128)
    pl.semaphore_wait(barrier, count)

    def sem(i):
        return sems.at[i]

    def n1(p, j):
        return p * 3 + j

    def nt(j):
        return 6 + j

    def n2(p, j, t):
        return 9 + (p * 3 + j) * 2 + t

    def n3(p, j, t):
        return 21 + (p * 3 + j) * 2 + t

    RB = 33

    def stage1(p):
        for j in range(3):
            ra = ROLES[j][0]
            me = pos[ra]
            src = data[p].at[:, pl.ds(OFF[j], WID[j])]
            for d in (1, 2, 3):
                dev = device(moved(pos, ra, d), core)
                if p == 0:
                    to = lax.rem(me + d, 4)
                    remote(tab.at[j, to], tabr.at[j, me], sem(nt(j)), sem(RB + nt(j)), dev).start()
                remote(src, ag[j].at[p, me], sem(n1(p, j)), sem(RB + n1(p, j)), dev).start()
            if p == 0:
                pltpu.make_async_copy(tab.at[j, me], tabr.at[j, me], sem(2 * RB + nt(j))).start()
            pltpu.make_async_copy(src, ag[j].at[p, me], sem(2 * RB + n1(p, j))).start()

    def wait1(p, j):
        if p == 0:
            dummy = tabr.at[j, pl.ds(0, 3)]
            done = remote(dummy, dummy, sem(nt(j)), sem(RB + nt(j)), device(pos, other))
            done.wait_recv()
            done.wait_send()
            pltpu.make_async_copy(tab.at[j, 0], tabr.at[j, 0], sem(2 * RB + nt(j))).wait()
        dummy = ag[j].at[p, pl.ds(0, 3)]
        done = remote(dummy, dummy, sem(n1(p, j)), sem(RB + n1(p, j)), device(pos, other))
        done.wait_recv()
        done.wait_send()
        dummy = ag[j].at[p, 0]
        pltpu.make_async_copy(dummy, dummy, sem(2 * RB + n1(p, j))).wait()

    sub3 = lax.broadcasted_iota(jnp.int32, (32, 8, 128), 1).astype(F32)

    def build_masks(j):
        wt_acc = jnp.zeros((32, 8, 1), F32)
        for a in range(4):
            code = tabr[j, a, 0].reshape(32, 1, 128)
            wgt = tabr[j, a, 1].reshape(32, 1, 128)
            code = jnp.broadcast_to(code, (32, 8, 128))
            wgt = jnp.broadcast_to(wgt, (32, 8, 128))
            hit = jnp.where(code == sub3, 1.0, 0.0)
            pm[j, a] = hit.reshape(256, 128).astype(BF16)
            wmain[j, a] = jnp.sum(hit * wgt, axis=2, keepdims=True).reshape(256, 1)
            for h in range(2):
                mine = jnp.where((code == 8.0) & (sub3 == float(h * 4 + a)), 1.0, 0.0)
                pm[j, 4 + h * 4 + a] = mine.reshape(256, 128).astype(BF16)
                wt_acc = wt_acc + jnp.sum(mine * wgt, axis=2, keepdims=True)
        wtail[j] = wt_acc.reshape(256, 1)

    def pack(p, j):
        half = WID[j] // 2

        def per_block(a, carry):
            for s, n in cols(j):
                res = jnp.dot(pm[j, a], ag[j][p, a, :, s : s + n], preferred_element_type=F32)
                if p == 0:
                    res = res * wmain[j, a]
                send2[j][p, :, :, a, :, s : s + n] = res.reshape(4, 8, 8, n).astype(BF16)
            return carry

        lax.fori_loop(0, 4, per_block, 0)
        for s in range(0, half, 128):
            res = jnp.zeros((256, 128), F32)
            for h in range(2):
                for a in range(4):
                    s0 = h * half + s
                    res = res + jnp.dot(
                        pm[j, 4 + h * 4 + a], ag[j][p, a, :, s0 : s0 + 128], preferred_element_type=F32
                    )
            if p == 0:
                res = res * wtail[j]
            send2t[j][p, :, :, :, s : s + 128] = res.reshape(4, 8, 8, 128).astype(BF16)

    def stage2(p, j):
        rb = ROLES[j][1]
        me = pos[rb]
        for d in (1, 2, 3):
            to = lax.rem(me + d, 4)
            dev = device(moved(pos, rb, d), core)
            remote(send2[j].at[p, to], recv2[j].at[p, me], sem(n2(p, j, 0)), sem(RB + n2(p, j, 0)), dev).start()
            remote(send2t[j].at[p, to], recv2t[j].at[p, me], sem(n2(p, j, 1)), sem(RB + n2(p, j, 1)), dev).start()

    def wait2(p, j):
        for t, ref in ((0, recv2), (1, recv2t)):
            dummy = ref[j].at[p, pl.ds(0, 3)]
            done = remote(dummy, dummy, sem(n2(p, j, t)), sem(RB + n2(p, j, t)), device(pos, other))
            done.wait_recv()
            done.wait_send()

    def stage3(p, j):
        ra, rb, rc = ROLES[j]
        for d in (0, 1, 2, 3):
            dst_pos = moved(pos, rc, d)
            for flip in (0, 1):
                k = core if flip == 0 else other
                ck = dst_pos[rc] * 2 + k
                for q in range(4):
                    b = lax.rem(pos[rb] + q, 4)
                    src = (send2 if q == 0 else recv2)[j].at[p, b, ck]
                    srct = (send2t if q == 0 else recv2t)[j].at[p, b, ck]
                    dst = main_at(mains[p], j, b, pos[rc], core)
                    dstt = tails[p][j].at[pos[rc] * 2 + core, b]
                    if d == 0 and flip == 0:
                        pltpu.make_async_copy(src, dst, sem(2 * RB + n3(p, j, 0))).start()
                        pltpu.make_async_copy(srct, dstt, sem(2 * RB + n3(p, j, 1))).start()
                    else:
                        dev = device(dst_pos, k)
                        remote(src, dst, sem(n3(p, j, 0)), sem(RB + n3(p, j, 0)), dev).start()
                        remote(srct, dstt, sem(n3(p, j, 1)), sem(RB + n3(p, j, 1)), dev).start()

    def wait3(p, j):
        for t, ref in ((0, send2), (1, send2t)):
            dummy = ref[j].at[p, :, pl.ds(0, 7)]
            done = remote(dummy, dummy, sem(n3(p, j, t)), sem(RB + n3(p, j, t)), device(pos, other))
            done.wait_recv()
            done.wait_send()
            dummy = ref[j].at[p, :, 0]
            pltpu.make_async_copy(dummy, dummy, sem(2 * RB + n3(p, j, t))).wait()

    stage1(0)
    stage1(1)
    for j in range(3):
        wait1(0, j)
        build_masks(j)
        pack(0, j)
        stage2(0, j)
    for j in range(3):
        wait1(1, j)
        pack(1, j)
    keep = pltpu.make_async_copy(pm, masks, sem(3 * RB))
    keep.start()
    for j in range(3):
        wait2(0, j)
        stage3(0, j)
    for j in range(3):
        stage2(1, j)
    for j in range(3):
        wait2(1, j)
        stage3(1, j)
    for p in range(2):
        for j in range(3):
            wait3(p, j)
    keep.wait()


def dispatch(ids_t, w_t, grad, rows):
    any_spec = pl.BlockSpec(memory_space=pl.ANY)
    vmem = pl.BlockSpec(memory_space=pltpu.VMEM)
    shape = jax.ShapeDtypeStruct
    main = shape((4, 4, 4, 2, 8, 4096), BF16)
    tails = [shape((8, 4, 8, w // 2), BF16) for w in WID]
    scratch = [pltpu.VMEM((2, 4, 128, w), BF16) for w in WID]
    scratch += [pltpu.VMEM((2, 4, 8, 4, 8, w), BF16) for w in WID] * 2
    scratch += [pltpu.VMEM((2, 4, 8, 8, w // 2), BF16) for w in WID] * 2
    scratch += [
        pltpu.VMEM((3, 4, 2, 32, 128), F32),
        pltpu.VMEM((3, 4, 2, 32, 128), F32),
        pltpu.VMEM((3, 12, 256, 128), BF16),
        pltpu.VMEM((3, 4, 256, 1), F32),
        pltpu.VMEM((3, 256, 1), F32),
        pltpu.SemaphoreType.DMA((100,)),
    ]
    return pl.pallas_call(
        dispatch_kernel,
        out_shape=[main, main] + tails + tails + [shape((3, 12, 256, 128), BF16)],
        in_specs=[vmem] * 4,
        out_specs=[any_spec] * 9,
        scratch_shapes=scratch,
        compiler_params=pltpu.CompilerParams(
            collective_id=0, has_side_effects=True, vmem_limit_bytes=62 << 20
        ),
        name="dispatch",
    )(ids_t, w_t, grad, rows)


def combine_kernel(*refs):
    main, t0, t1, t2, masks, out = refs[:6]
    tails = (t0, t1, t2)
    scratch = refs[6:]
    r1 = scratch[0:3]
    r2 = scratch[3:6]
    r1t = scratch[6:9]
    r2t = scratch[9:12]
    part = scratch[12:15]
    got = scratch[15:18]
    own = scratch[18]
    sems = scratch[19]
    pos, core = coords()
    other = 1 - core
    barrier, count = greet(pos, core)
    pl.semaphore_wait(barrier, count)
    RB = 15

    def sem(i):
        return sems.at[i]

    def n1(j, t):
        return j * 2 + t

    def n2(j, t):
        return 6 + j * 2 + t

    def n3(j):
        return 12 + j

    def stage1(j):
        ra, rb, rc = ROLES[j]
        mine = pos[rc] * 2 + core
        for d in (0, 1, 2, 3):
            dst_pos = moved(pos, rc, d)
            for flip in (0, 1):
                k = core if flip == 0 else other
                ck = dst_pos[rc] * 2 + k
                for b in range(4):
                    src = main_at(main, j, b, dst_pos[rc], k)
                    dst = r1[j].at[b, mine]
                    if d == 0 and flip == 0:
                        pltpu.make_async_copy(src, dst, sem(2 * RB + n1(j, 0))).start()
                    else:
                        remote(src, dst, sem(n1(j, 0)), sem(RB + n1(j, 0)), device(dst_pos, k)).start()
                src = tails[j].at[ck]
                dst = r1t[j].at[:, mine]
                if d == 0 and flip == 0:
                    pltpu.make_async_copy(src, dst, sem(2 * RB + n1(j, 1))).start()
                else:
                    remote(src, dst, sem(n1(j, 1)), sem(RB + n1(j, 1)), device(dst_pos, k)).start()

    def wait1(j):
        for t, ref in ((0, r1), (1, r1t)):
            dummy = ref[j].at[:, pl.ds(0, 7)]
            done = remote(dummy, dummy, sem(n1(j, t)), sem(RB + n1(j, t)), device(pos, other))
            done.wait_recv()
            done.wait_send()
            dummy = ref[j].at[:, 0]
            pltpu.make_async_copy(dummy, dummy, sem(2 * RB + n1(j, t))).wait()

    def stage2(j):
        rb = ROLES[j][1]
        me = pos[rb]
        for t, (a, b) in enumerate(((r1, r2), (r1t, r2t))):
            for d in (1, 2, 3):
                to = lax.rem(me + d, 4)
                dev = device(moved(pos, rb, d), core)
                remote(a[j].at[to], b[j].at[me], sem(n2(j, t)), sem(RB + n2(j, t)), dev).start()
            pltpu.make_async_copy(a[j].at[me], b[j].at[me], sem(2 * RB + n2(j, t))).start()

    def wait2(j):
        for t, ref in ((0, r2), (1, r2t)):
            dummy = ref[j].at[pl.ds(0, 3)]
            done = remote(dummy, dummy, sem(n2(j, t)), sem(RB + n2(j, t)), device(pos, other))
            done.wait_recv()
            done.wait_send()
            dummy = ref[j].at[0]
            pltpu.make_async_copy(dummy, dummy, sem(2 * RB + n2(j, t))).wait()

    def fold(j):
        ra = ROLES[j][0]
        half = WID[j] // 2
        for d in range(4):
            a = lax.rem(pos[ra] + d, 4)
            mt = masks[j, a]
            for s in range(0, half, 128):
                tail = r2t[j][:, :, :, s : s + 128].astype(F32).reshape(256, 128).astype(BF16)
                for h in range(2):
                    s0 = h * half + s
                    rows = r2[j][:, :, a, :, s0 : s0 + 128].astype(F32).reshape(256, 128).astype(BF16)
                    res = lax.dot_general(mt, rows, (((0,), (0,)), ((), ())), preferred_element_type=F32)
                    res = res + lax.dot_general(
                        masks[j, 4 + h * 4 + a], tail, (((0,), (0,)), ((), ())), preferred_element_type=F32
                    )
                    if d == 0:
                        own[:, OFF[j] + s0 : OFF[j] + s0 + 128] = res
                    else:
                        part[j][d - 1, :, s0 : s0 + 128] = res.astype(BF16)

    def stage3(j):
        ra = ROLES[j][0]
        for d in (1, 2, 3):
            dev = device(moved(pos, ra, d), core)
            remote(part[j].at[d - 1], got[j].at[d - 1], sem(n3(j)), sem(RB + n3(j)), dev).start()

    def finish(j):
        dummy = got[j]
        done = remote(dummy, dummy, sem(n3(j)), sem(RB + n3(j)), device(pos, other))
        done.wait_recv()
        done.wait_send()
        for s, n in cols(j):
            total = own[:, OFF[j] + s : OFF[j] + s + n]
            for d in range(3):
                total = total + got[j][d, :, s : s + n].astype(F32)
            out[:, OFF[j] + s : OFF[j] + s + n] = total.astype(BF16)

    for j in range(3):
        stage1(j)
    for j in range(3):
        wait1(j)
        stage2(j)
    for j in range(3):
        wait2(j)
        fold(j)
        stage3(j)
    for j in range(3):
        finish(j)


def combine(main, tails, masks):
    any_spec = pl.BlockSpec(memory_space=pl.ANY)
    vmem = pl.BlockSpec(memory_space=pltpu.VMEM)
    scratch = [pltpu.VMEM((4, 8, 4, 8, w), BF16) for w in WID] * 2
    scratch += [pltpu.VMEM((4, 8, 8, w // 2), BF16) for w in WID] * 2
    scratch += [pltpu.VMEM((3, 128, w), BF16) for w in WID] * 2
    scratch += [pltpu.VMEM((128, 4096), F32), pltpu.SemaphoreType.DMA((45,))]
    return pl.pallas_call(
        combine_kernel,
        out_shape=jax.ShapeDtypeStruct((128, 4096), BF16),
        in_specs=[any_spec] * 4 + [vmem],
        out_specs=vmem,
        scratch_shapes=scratch,
        compiler_params=pltpu.CompilerParams(
            collective_id=1, has_side_effects=True, vmem_limit_bytes=62 << 20
        ),
        name="combine",
    )(main, *tails, masks)


def tail_rows(j):
    i = jnp.arange(256, dtype=jnp.int32)
    ra, rb, rc = ROLES[j]
    v = [None] * 3
    v[rc] = i // 64
    v[rb] = (i // 8) % 4
    v[ra] = i % 4
    block = ((v[0] * 4 + v[1]) * 4 + v[2]) * 2 + (i // 32) % 2
    half = (i // 4) % 2
    return block, half


def unpack_tails(tails):
    parts = []
    blocks = jnp.arange(128, dtype=jnp.int32)
    for j in range(3):
        block, half = tail_rows(j)
        flat = tails[j].reshape(256, WID[j] // 2)
        for h in range(2):
            pick = ((blocks[:, None] == block[None, :]) & (half[None, :] == h)).astype(BF16)
            parts.append(jnp.dot(pick, flat, preferred_element_type=F32).astype(BF16))
    return jnp.concatenate(parts, axis=1)


def pack_tails(tail):
    packed = []
    blocks = jnp.arange(128, dtype=jnp.int32)
    for j in range(3):
        block, half = tail_rows(j)
        w = WID[j] // 2
        same = block[:, None] == blocks[None, :]
        picks = [(same & (half[:, None] == h)).astype(BF16) for h in range(2)]
        lo = tail[:, OFF[j] : OFF[j] + w]
        hi = tail[:, OFF[j] + w : OFF[j] + 2 * w]
        res = jnp.dot(picks[0], lo, preferred_element_type=F32) + jnp.dot(
            picks[1], hi, preferred_element_type=F32
        )
        packed.append(res.astype(BF16).reshape(8, 4, 8, w))
    return packed


def canonical_slots():
    i = jnp.arange(1152, dtype=jnp.int32)
    is_tail = i >= 1024
    block = jnp.where(is_tail, i - 1024, i // 8)
    r = jnp.where(is_tail, 8, i % 8)
    x, y, z, k = block // 32, (block // 8) % 4, (block // 2) % 4, block % 2
    b = ((y * 2 + z % 2) * 4 + x) * 4 + (z // 2) * 2 + k
    return b * 9 + r


def mm(a, b, da, db):
    return lax.dot_general(a, b, (((da,), (db,)), ((), ())), preferred_element_type=F32)


def expert_backward(parts_g, parts_x, pre, wg, wu, wd, ga, go, ua, uo, da, do):
    outs = []
    sums = [0.0] * 5
    both_in = jnp.concatenate([ga, ua], axis=0)
    for g, x, (gate_pre, up_pre) in zip(parts_g, parts_x, pre):
        gate = gate_pre.astype(F32)
        up = up_pre.astype(F32)
        sig = jax.nn.sigmoid(gate)
        silu = gate * sig
        hidden = (silu * up).astype(BF16)
        down_lora = mm(hidden, da, 1, 1).astype(BF16)
        grad_lora = mm(g, do, 1, 1).astype(BF16)
        sums[0] = sums[0] + mm(down_lora, g, 0, 0)
        sums[1] = sums[1] + mm(grad_lora, hidden, 0, 0)
        gh = mm(g, wd, 1, 1) + adapter_scale * mm(grad_lora, da, 1, 0)
        gg = (gh * up * sig * (1.0 + gate * (1.0 - sig))).astype(BF16)
        gu = (gh * silu).astype(BF16)
        deltas = mm(x, both_in, 1, 1).astype(BF16)
        sums[2] = sums[2] + mm(deltas[:, :16], gg, 0, 0)
        sums[3] = sums[3] + mm(deltas[:, 16:], gu, 0, 0)
        back = jnp.concatenate([mm(gg, go, 1, 1).astype(BF16), mm(gu, uo, 1, 1).astype(BF16)], axis=1)
        sums[4] = sums[4] + mm(back, x, 0, 0)
        left = jnp.concatenate([gg, gu, back], axis=1)
        right = jnp.concatenate([wg, wu, (both_in.astype(F32) * adapter_scale).astype(BF16).T], axis=1)
        outs.append(mm(left, right, 1, 1).astype(BF16))
    r = [(adapter_scale * s).astype(BF16) for s in sums]
    return outs, (r[4][:16], r[2], r[4][16:], r[3], r[1], r[0])


def local(rows, grad, choice, weight, wg, wu, wd, ga, go, ua, uo, da, do, gate_pre, up_pre):
    res = dispatch(choice.T, weight.T, grad, rows)
    gmain, xmain = res[0].reshape(1024, 4096), res[1].reshape(1024, 4096)
    gtail, xtail = unpack_tails(res[2:5]), unpack_tails(res[5:8])
    masks = res[8]
    order = (canonical_slots()[:, None] == jnp.arange(1152, dtype=jnp.int32)[None, :]).astype(BF16)
    gp = jnp.dot(order, gate_pre[0], preferred_element_type=F32).astype(BF16)
    up = jnp.dot(order, up_pre[0], preferred_element_type=F32).astype(BF16)
    outs, grads = expert_backward(
        (gmain, gtail),
        (xmain, xtail),
        ((gp[:1024], up[:1024]), (gp[1024:], up[1024:])),
        wg[0], wu[0], wd[0], ga[0], go[0], ua[0], uo[0], da[0], do[0],
    )
    grad_in = combine(outs[0].reshape(4, 4, 4, 2, 8, 4096), pack_tails(outs[1]), masks)
    return (grad_in,) + tuple(v[None] for v in grads)


def solution(mesh):
    row = P(("ctx", "ep"), None)
    cube = P(("ctx", "ep"), None, None)
    return jax.shard_map(
        local,
        mesh=mesh,
        in_specs=(row,) * 4 + (cube,) * 11,
        out_specs=(row,) + (cube,) * 6,
        check_vma=False,
    )
```

```python
import jax
import jax.numpy as jnp
from jax import lax
from jax.experimental import pallas as pl
from jax.experimental.pallas import tpu as pltpu
from jax.sharding import PartitionSpec as P

MESH = pl.DeviceIdType.MESH
ROLES = ((0, 1, 2), (1, 2, 0), (2, 0, 1))
WID = (1280, 1280, 1536)
OFF = (0, 1280, 2560)
CHUNK = 256
F32 = jnp.float32
BF16 = jnp.bfloat16
adapter_scale = 2.0


def coords():
    c = lax.axis_index("ctx")
    e = lax.axis_index("ep")
    x = lax.rem(c, 4)
    y = c // 8
    z = (e // 2) * 2 + lax.rem(c // 4, 2)
    return (x, y, z), lax.rem(e, 2)


def device(pos, core):
    x, y, z = pos
    return ((y * 2 + lax.rem(z, 2)) * 4 + x, (z // 2) * 2 + core)


def moved(pos, axis, d):
    out = list(pos)
    out[axis] = lax.rem(pos[axis] + d, 4)
    return tuple(out)


def greet(pos, core):
    barrier = pltpu.get_barrier_semaphore()
    other = 1 - core
    peers = [device(pos, other)]
    for axis in range(3):
        for d in (1, 2, 3):
            peers.append(device(moved(pos, axis, d), core))
            peers.append(device(moved(pos, axis, d), other))
    for peer in peers:
        pl.semaphore_signal(barrier, inc=1, device_id=peer, device_id_type=MESH)
    return barrier, len(peers)


def remote(src, dst, ssem, rsem, dev):
    return pltpu.make_async_remote_copy(
        src_ref=src, dst_ref=dst, send_sem=ssem, recv_sem=rsem, device_id=dev, device_id_type=MESH
    )


def expert_ids(j, shape):
    i = lax.broadcasted_iota(jnp.int32, shape, 0)
    v = [None] * 3
    a, b, c = ROLES[j]
    v[a] = i // 32
    v[b] = (i // 8) % 4
    v[c] = (i // 2) % 4
    k = i % 2
    x, y, z = v
    return ((y * 2 + z % 2) * 4 + x) * 4 + (z // 2) * 2 + k


def main_at(ref, j, b, c, k):
    ra, rb, rc = ROLES[j]
    idx = [None] * 3
    idx[ra] = slice(None)
    idx[rb] = b
    idx[rc] = c
    return ref.at[idx[0], idx[1], idx[2], k, :, pl.ds(OFF[j], WID[j])]


def cols(j):
    return [(s, CHUNK) for s in range(0, WID[j], CHUNK)]


def rows_of(i):
    out = []
    for j in range(3):
        ra, rb, rc = ROLES[j]
        v = [None] * 3
        v[rc] = i // 64
        v[rb] = (i // 8) % 4
        v[ra] = i % 4
        out.append((((v[0] * 4 + v[1]) * 4 + v[2]) * 2 + (i // 32) % 2, (i // 4) % 2))
    return out


def slot_of(block, r):
    x, y, z, k = block // 32, (block // 8) % 4, (block // 2) % 4, block % 2
    return (((y * 2 + z % 2) * 4 + x) * 4 + (z // 2) * 2 + k) * 9 + r


def mm(a, b, da, db):
    return lax.dot_general(a, b, (((da,), (db,)), ((), ())), preferred_element_type=F32)


def flat(v):
    n = v.shape[-1]
    return v.astype(F32).reshape(-1, n).astype(BF16)


N_IN = 15
N_OUT = 7
N_TMP = 27


def block_kernel(*refs):
    (ids_ref, wt_ref, g_hbm, x_hbm, gate_hbm, up_hbm, wg_hbm, wu_hbm, wd_hbm, ga, go, ua, uo, da, do) = refs[:N_IN]
    out, o_gi, o_go, o_ui, o_uo, o_di, o_do = refs[N_IN : N_IN + N_OUT]
    tmp = refs[N_IN + N_OUT : N_IN + N_OUT + N_TMP]
    gmain, xmain, rmain = tmp[0:3]
    tails = (tmp[3:6], tmp[6:9])
    rtails = tmp[9:12]
    recv2, recv2t = tmp[12:15], tmp[15:18]
    r1, r1t = tmp[18:21], tmp[21:24]
    r2t_hbm = tmp[24:27]
    sc = refs[N_IN + N_OUT + N_TMP :]
    ag, send2, send2t, r2, got = sc[0:3], sc[3:6], sc[6:9], sc[9:12], sc[12:15]
    (tab, tabr, pm, wmain, wtail, own, gg, gu, gtail, dlora, back, acc_do, acc_di, acc_in, acc_o, wide, narrow, sems, rsems, lsems) = sc[15:]
    mains = (gmain, xmain)
    data = (g_hbm, x_hbm)
    pos, core = coords()
    other = 1 - core
    barrier, count = greet(pos, core)

    row = lax.broadcasted_iota(jnp.int32, (128, 128), 0)
    lane = lax.broadcasted_iota(jnp.int32, (128, 128), 1)
    strict = (row < lane).astype(BF16)
    for j in range(3):
        eid = expert_ids(j, (128, 128))
        hit = jnp.zeros((128, 128), F32)
        wgt = jnp.zeros((128, 128), F32)
        for k in range(8):
            same = eid == ids_ref[k : k + 1, :]
            hit = hit + jnp.where(same, 1.0, 0.0)
            wgt = wgt + jnp.where(same, wt_ref[k : k + 1, :], 0.0)
        rank = jnp.dot(hit.astype(BF16), strict, preferred_element_type=F32)
        code = jnp.where(hit > 0.5, rank, -1.0)
        tab[j, :, 0] = code.reshape(4, 32, 128)
        tab[j, :, 1] = wgt.reshape(4, 32, 128)
    pl.semaphore_wait(barrier, count)

    def sem(i):
        return sems.at[i]

    def n1(p, j):
        return p * 3 + j

    def nt(j):
        return 6 + j

    def n2(p, j, t):
        return 9 + (p * 3 + j) * 2 + t

    def n3(p, j, t):
        return 21 + (p * 3 + j) * 2 + t

    RB = 33

    def settle(dummy, ssem, rsem):
        done = remote(dummy, dummy, ssem, rsem, device(pos, other))
        done.wait_recv()
        done.wait_send()

    def here(src, dst, s):
        return pltpu.make_async_copy(src, dst, s)

    def stage1(p):
        for j in range(3):
            ra = ROLES[j][0]
            me = pos[ra]
            src = data[p].at[:, pl.ds(OFF[j], WID[j])]
            for d in (1, 2, 3):
                dev = device(moved(pos, ra, d), core)
                if p == 0:
                    to = lax.rem(me + d, 4)
                    remote(tab.at[j, to], tabr.at[j, me], sem(nt(j)), sem(RB + nt(j)), dev).start()
                remote(src, ag[j].at[p, me], sem(n1(p, j)), sem(RB + n1(p, j)), dev).start()
            if p == 0:
                here(tab.at[j, me], tabr.at[j, me], sem(2 * RB + nt(j))).start()
            here(src, ag[j].at[p, me], sem(2 * RB + n1(p, j))).start()

    def wait1(p, j):
        if p == 0:
            settle(tabr.at[j, pl.ds(0, 3)], sem(nt(j)), sem(RB + nt(j)))
            here(tab.at[j, 0], tabr.at[j, 0], sem(2 * RB + nt(j))).wait()
        settle(ag[j].at[p, pl.ds(0, 3)], sem(n1(p, j)), sem(RB + n1(p, j)))
        here(ag[j].at[p, 0], ag[j].at[p, 0], sem(2 * RB + n1(p, j))).wait()

    sub3 = lax.broadcasted_iota(jnp.int32, (32, 8, 128), 1).astype(F32)

    def build_masks(j):
        wt_acc = jnp.zeros((32, 8, 1), F32)
        for a in range(4):
            code = jnp.broadcast_to(tabr[j, a, 0].reshape(32, 1, 128), (32, 8, 128))
            wgt = jnp.broadcast_to(tabr[j, a, 1].reshape(32, 1, 128), (32, 8, 128))
            hit = jnp.where(code == sub3, 1.0, 0.0)
            pm[j, a] = hit.reshape(256, 128).astype(BF16)
            wmain[j, a] = jnp.sum(hit * wgt, axis=2, keepdims=True).reshape(256, 1)
            for h in range(2):
                mine = jnp.where((code == 8.0) & (sub3 == float(h * 4 + a)), 1.0, 0.0)
                pm[j, 4 + h * 4 + a] = mine.reshape(256, 128).astype(BF16)
                wt_acc = wt_acc + jnp.sum(mine * wgt, axis=2, keepdims=True)
        wtail[j] = wt_acc.reshape(256, 1)

    def pack(p, j):
        half = WID[j] // 2

        def per_block(a, carry):
            for s, n in cols(j):
                res = jnp.dot(pm[j, a], ag[j][p, a, :, s : s + n], preferred_element_type=F32)
                if p == 0:
                    res = res * wmain[j, a]
                send2[j][:, :, a, :, s : s + n] = res.reshape(4, 8, 8, n).astype(BF16)
            return carry

        lax.fori_loop(0, 4, per_block, 0)

        def per_cols(i, carry):
            s = pl.multiple_of(i * 128, 128)
            res = jnp.zeros((256, 128), F32)
            for h in range(2):
                for a in range(4):
                    src = ag[j][p, a, :, pl.ds(pl.multiple_of(h * half + s, 128), 128)]
                    res = res + jnp.dot(pm[j, 4 + h * 4 + a], src, preferred_element_type=F32)
            if p == 0:
                res = res * wtail[j]
            send2t[j][:, :, :, pl.ds(s, 128)] = res.reshape(4, 8, 8, 128).astype(BF16)
            return carry

        lax.fori_loop(0, half // 128, per_cols, 0)

    def stage2(p, j):
        rb = ROLES[j][1]
        me = pos[rb]
        for t, (a, b) in enumerate(((send2, recv2), (send2t, recv2t))):
            for d in (1, 2, 3):
                to = lax.rem(me + d, 4)
                dev = device(moved(pos, rb, d), core)
                remote(a[j].at[to], b[j].at[p, me], sem(n2(p, j, t)), sem(RB + n2(p, j, t)), dev).start()
            here(a[j].at[me], b[j].at[p, me], sem(2 * RB + n2(p, j, t))).start()

    def wait2(p, j):
        for t, ref in ((0, recv2), (1, recv2t)):
            settle(ref[j].at[p, pl.ds(0, 3)], sem(n2(p, j, t)), sem(RB + n2(p, j, t)))
            here(ref[j].at[p, 0], ref[j].at[p, 0], sem(2 * RB + n2(p, j, t))).wait()

    def stage3(p, j):
        ra, rb, rc = ROLES[j]
        for d in (1, 2, 3, 0):
            dst_pos = moved(pos, rc, d)
            for flip in (0, 1):
                k = core if flip == 0 else other
                ck = dst_pos[rc] * 2 + k
                dev = device(dst_pos, k)
                for b in range(4):
                    src = recv2[j].at[p, b, ck]
                    dst = main_at(mains[p], j, b, pos[rc], core)
                    if d == 0 and flip == 0:
                        here(src, dst, sem(2 * RB + n3(p, j, 0))).start()
                    else:
                        remote(src, dst, sem(n3(p, j, 0)), sem(RB + n3(p, j, 0)), dev).start()
                src = recv2t[j].at[p, :, ck]
                dst = tails[p][j].at[pos[rc] * 2 + core]
                if d == 0 and flip == 0:
                    here(src, dst, sem(2 * RB + n3(p, j, 1))).start()
                else:
                    remote(src, dst, sem(n3(p, j, 1)), sem(RB + n3(p, j, 1)), dev).start()

    def wait3(p, j):
        for t, ref in ((0, recv2), (1, recv2t)):
            settle(ref[j].at[p, :, pl.ds(0, 7)], sem(n3(p, j, t)), sem(RB + n3(p, j, t)))
            dummy = ref[j].at[p, :, 0]
            here(dummy, dummy, sem(2 * RB + n3(p, j, t))).wait()

    RR = 15

    def rsem(i):
        return rsems.at[i]

    def m1(j, t):
        return j * 2 + t

    def m2(j, t):
        return 6 + j * 2 + t

    def back1(j):
        ra, rb, rc = ROLES[j]
        mine = pos[rc] * 2 + core
        for d in (1, 2, 3, 0):
            dst_pos = moved(pos, rc, d)
            for flip in (0, 1):
                k = core if flip == 0 else other
                ck = dst_pos[rc] * 2 + k
                dev = device(dst_pos, k)
                local_copy = d == 0 and flip == 0
                for b in range(4):
                    src = main_at(rmain, j, b, dst_pos[rc], k)
                    dst = r1[j].at[b, mine]
                    if local_copy:
                        here(src, dst, rsem(2 * RR + m1(j, 0))).start()
                    else:
                        remote(src, dst, rsem(m1(j, 0)), rsem(RR + m1(j, 0)), dev).start()
                src = rtails[j].at[ck]
                dst = r1t[j].at[:, mine]
                if local_copy:
                    here(src, dst, rsem(2 * RR + m1(j, 1))).start()
                else:
                    remote(src, dst, rsem(m1(j, 1)), rsem(RR + m1(j, 1)), dev).start()

    def back_wait1(j):
        for t, ref in ((0, r1), (1, r1t)):
            settle(ref[j].at[:, pl.ds(0, 7)], rsem(m1(j, t)), rsem(RR + m1(j, t)))
            dummy = ref[j].at[:, 0]
            here(dummy, dummy, rsem(2 * RR + m1(j, t))).wait()

    def back2(j):
        rb = ROLES[j][1]
        me = pos[rb]
        for t, (a, b) in enumerate(((r1, r2), (r1t, r2t_hbm))):
            for d in (1, 2, 3):
                to = lax.rem(me + d, 4)
                dev = device(moved(pos, rb, d), core)
                remote(a[j].at[to], b[j].at[me], rsem(m2(j, t)), rsem(RR + m2(j, t)), dev).start()
            here(a[j].at[me], b[j].at[me], rsem(2 * RR + m2(j, t))).start()

    def back_wait2(j):
        for t, ref in ((0, r2), (1, r2t_hbm)):
            settle(ref[j].at[pl.ds(0, 3)], rsem(m2(j, t)), rsem(RR + m2(j, t)))
            here(ref[j].at[0], ref[j].at[0], rsem(2 * RR + m2(j, t))).wait()

    def fold(j):
        ra = ROLES[j][0]
        half = WID[j] // 2
        cp = here(r2t_hbm[j], send2t[j], lsems.at[0])
        cp.start()
        cp.wait()

        def per_cols(i, carry):
            s = pl.multiple_of(i * 128, 128)
            tail = flat(send2t[j][:, :, :, pl.ds(s, 128)])
            for d in range(4):
                a = lax.rem(pos[ra] + d, 4)
                for h in range(2):
                    s0 = pl.multiple_of(h * half + s, 128)
                    rows = flat(r2[j][:, :, a, :, pl.ds(s0, 128)])
                    res = mm(pm[j, a], rows, 0, 0) + mm(pm[j, 4 + h * 4 + a], tail, 0, 0)
                    if d == 0:
                        own[:, pl.ds(pl.multiple_of(OFF[j] + s0, 128), 128)] = res
                    else:
                        ag[j][1, d - 1, :, pl.ds(s0, 128)] = res.astype(BF16)
            return carry

        lax.fori_loop(0, half // 128, per_cols, 0)

    def back3(j):
        ra = ROLES[j][0]
        for d in (1, 2, 3):
            dev = device(moved(pos, ra, d), core)
            remote(ag[j].at[1, d - 1], got[j].at[d - 1], rsem(12 + j), rsem(RR + 12 + j), dev).start()

    def finish(j):
        settle(got[j], rsem(12 + j), rsem(RR + 12 + j))
        for s, n in cols(j):
            total = own[:, OFF[j] + s : OFF[j] + s + n]
            for d in range(3):
                total = total + got[j][d, :, s : s + n].astype(F32)
            out[:, OFF[j] + s : OFF[j] + s + n] = total.astype(BF16)

    def tail_picks(j, swap):
        shape = (256, 128) if swap else (128, 256)
        i = lax.broadcasted_iota(jnp.int32, shape, 0 if swap else 1)
        n = lax.broadcasted_iota(jnp.int32, shape, 1 if swap else 0)
        block, half = rows_of(i)[j]
        return [jnp.where((block == n) & (half == h), 1.0, 0.0).astype(BF16) for h in range(2)]

    def load_tail(p, dst, stage):
        for j in range(3):
            w = WID[j] // 2
            cp = here(tails[p][j], stage.at[:, :, :, pl.ds(0, w)], lsems.at[0])
            cp.start()
            cp.wait()
            picks = tail_picks(j, False)
            for s in range(0, w, 128):
                rows = flat(stage[:, :, :, s : s + 128])
                for h in range(2):
                    o = OFF[j] + h * w + s
                    dst[0:128, o : o + 128] = mm(picks[h], rows, 1, 0).astype(BF16)

    wide[0:16] = ga[...]
    wide[16:32] = ua[...]
    narrow[0, 0:16] = go[...]
    narrow[0, 16:32] = jnp.zeros_like(go)
    narrow[1, 0:16] = jnp.zeros_like(uo)
    narrow[1, 16:32] = uo[...]
    for ref in (acc_do, acc_di, acc_in, acc_o):
        ref[...] = jnp.zeros_like(ref)

    stage1(0)
    stage1(1)
    for j in range(3):
        wait1(0, j)
        build_masks(j)
        pack(0, j)
        stage2(0, j)
    for j in range(3):
        wait2(0, j)
        stage3(0, j)

    def first_half(gate_pre, up_pre, wd, slab, gc, stage):
        loads = [
            here(gate_hbm, gate_pre, lsems.at[1]),
            here(up_hbm, up_pre, lsems.at[2]),
            here(wd_hbm, wd, lsems.at[3]),
        ]
        for cp in loads:
            cp.start()
        for j in range(3):
            wait1(1, j)
            pack(1, j)
            stage2(1, j)
        for cp in loads:
            cp.wait()
        for j in range(3):
            wait3(0, j)

        def rows_at(r0, n, order):
            gate = jnp.dot(order, gate_pre[...], preferred_element_type=F32)
            up = jnp.dot(order, up_pre[...], preferred_element_type=F32)
            sig = jax.nn.sigmoid(gate)
            silu = gate * sig
            hidden = (silu * up).astype(BF16)
            g = gc[0:n]
            dlora[pl.ds(r0, n)] = mm(hidden, da[...], 1, 1).astype(BF16)
            gl = mm(g, do[...], 1, 1).astype(BF16)
            acc_di[...] += mm(gl, hidden, 0, 0)
            gh = mm(g, wd[...], 1, 1) + adapter_scale * mm(gl, da[...], 1, 0)
            gate_grad = (gh * up * sig * (1.0 + gate * (1.0 - sig))).astype(BF16)
            up_grad = (gh * silu).astype(BF16)
            gg[pl.ds(r0, n)] = gate_grad
            gu[pl.ds(r0, n)] = up_grad
            both = mm(gate_grad, narrow[0], 1, 1) + mm(up_grad, narrow[1], 1, 1)
            back[pl.ds(r0, n)] = both.astype(BF16)

        def main_rows(c, carry):
            cp = here(gmain.at[c], slab, lsems.at[0])
            cp.start()
            i = lax.broadcasted_iota(jnp.int32, (256, 1152), 0)
            n = lax.broadcasted_iota(jnp.int32, (256, 1152), 1)
            order = jnp.where(slot_of(c * 32 + i // 8, i % 8) == n, 1.0, 0.0).astype(BF16)
            cp.wait()
            for s in range(0, 4096, 512):
                gc[:, s : s + 512] = flat(slab[:, :, :, :, s : s + 512])
            rows_at(pl.multiple_of(c * 256, 256), 256, order)
            return carry

        lax.fori_loop(0, 4, main_rows, 0)
        for j in range(3):
            wait2(1, j)
            stage3(1, j)
        load_tail(0, gtail, stage)
        i = lax.broadcasted_iota(jnp.int32, (128, 1152), 0)
        n = lax.broadcasted_iota(jnp.int32, (128, 1152), 1)
        gc[0:128] = gtail[...]
        rows_at(1024, 128, jnp.where(slot_of(i, 8) == n, 1.0, 0.0).astype(BF16))

    pl.run_scoped(
        first_half,
        pltpu.VMEM((1152, 768), BF16),
        pltpu.VMEM((1152, 768), BF16),
        pltpu.VMEM((768, 4096), BF16),
        pltpu.VMEM((4, 4, 2, 8, 4096), BF16),
        pltpu.VMEM((256, 4096), BF16),
        pltpu.VMEM((8, 4, 8, 768), BF16),
    )

    def second_half(wgu, ro, tail_out, tail_pack):
        for j in range(3):
            w = WID[j]
            half = w // 2
            loads = [
                here(src.at[pl.ds(OFF[j], w)], wgu.at[t, pl.ds(0, w)], lsems.at[1 + t])
                for t, src in enumerate((wg_hbm, wu_hbm))
            ]
            for cp in loads:
                cp.start()
            for cp in loads:
                cp.wait()

            def per_cols(i, carry):
                s = pl.multiple_of(i * CHUNK, CHUNK)
                o = pl.multiple_of(OFF[j] + s, CHUNK)
                slot = lax.rem(i, 2)

                def rows(r0, n):
                    res = mm(gg[r0 : r0 + n], wgu[0, pl.ds(s, CHUNK)], 1, 1)
                    res = res + mm(gu[r0 : r0 + n], wgu[1, pl.ds(s, CHUNK)], 1, 1)
                    return res + adapter_scale * mm(back[r0 : r0 + n], wide[:, pl.ds(o, CHUNK)], 1, 0)

                @pl.when(i >= 2)
                def _():
                    here(ro.at[0], rmain.at[:, :, :, :, :, pl.ds(0, CHUNK)], lsems.at[3 + slot]).wait()

                for x in range(4):
                    ro[slot, x] = rows(x * 256, 256).reshape(4, 4, 2, 8, CHUNK).astype(BF16)
                tail_out[:, pl.ds(s, CHUNK)] = rows(1024, 128).astype(BF16)
                here(ro.at[slot], rmain.at[:, :, :, :, :, pl.ds(o, CHUNK)], lsems.at[3 + slot]).start()
                return carry

            lax.fori_loop(0, w // CHUNK, per_cols, 0)
            picks = tail_picks(j, True)
            for s in range(0, half, 128):
                res = mm(picks[0], tail_out[:, s : s + 128], 1, 0)
                res = res + mm(picks[1], tail_out[:, half + s : half + s + 128], 1, 0)
                tail_pack[:, :, :, s : s + 128] = res.reshape(8, 4, 8, 128).astype(BF16)
            cp = here(tail_pack.at[:, :, :, pl.ds(0, half)], rtails[j], lsems.at[0])
            cp.start()
            for slot in range(2):
                here(ro.at[0], rmain.at[:, :, :, :, :, pl.ds(0, CHUNK)], lsems.at[3 + slot]).wait()
            cp.wait()
            back1(j)

    pl.run_scoped(
        second_half,
        pltpu.VMEM((2, 1536, 768), BF16),
        pltpu.VMEM((2, 4, 4, 4, 2, 8, CHUNK), BF16),
        pltpu.VMEM((128, 1536), BF16),
        pltpu.VMEM((8, 4, 8, 768), BF16),
    )

    for j in range(3):
        wait3(1, j)

    def adapters(slab, xc, gc, stage):
        def add(r0, n, g, x):
            deltas = mm(x, wide[...], 1, 1).astype(BF16)
            acc_o[0] += mm(deltas, gg[pl.ds(r0, n)], 0, 0)
            acc_o[1] += mm(deltas, gu[pl.ds(r0, n)], 0, 0)
            lora = back[pl.ds(r0, n)]
            down = dlora[pl.ds(r0, n)]
            acc_in[...] += mm(lora, x, 0, 0)
            acc_do[...] += mm(down, g, 0, 0)

        def main_rows(c, carry):
            cps = [here(gmain.at[c], slab.at[0], lsems.at[1]), here(xmain.at[c], slab.at[1], lsems.at[2])]
            for cp in cps:
                cp.start()
            for cp in cps:
                cp.wait()
            for s in range(0, 4096, 512):
                gc[:, s : s + 512] = flat(slab[0, :, :, :, :, s : s + 512])
                xc[:, s : s + 512] = flat(slab[1, :, :, :, :, s : s + 512])
            add(pl.multiple_of(c * 256, 256), 256, gc[...], xc[...])
            return carry

        lax.fori_loop(0, 4, main_rows, 0)
        for j in range(3):
            back_wait1(j)
            back2(j)
        load_tail(1, xc, stage)
        add(1024, 128, gtail[...], xc[0:128])

    pl.run_scoped(
        adapters,
        pltpu.VMEM((2, 4, 4, 2, 8, 4096), BF16),
        pltpu.VMEM((256, 4096), BF16),
        pltpu.VMEM((256, 4096), BF16),
        pltpu.VMEM((8, 4, 8, 768), BF16),
    )
    o_gi[...] = (adapter_scale * acc_in[0:16]).astype(BF16)
    o_ui[...] = (adapter_scale * acc_in[16:32]).astype(BF16)
    o_go[...] = (adapter_scale * acc_o[0, 0:16]).astype(BF16)
    o_uo[...] = (adapter_scale * acc_o[1, 16:32]).astype(BF16)
    o_di[...] = (adapter_scale * acc_di[...]).astype(BF16)
    o_do[...] = (adapter_scale * acc_do[...]).astype(BF16)

    for j in range(3):
        back_wait2(j)
        fold(j)
        back3(j)
    for j in range(3):
        finish(j)


def whole_block(*operands):
    any_spec = pl.BlockSpec(memory_space=pl.ANY)
    vmem = pl.BlockSpec(memory_space=pltpu.VMEM)

    def shape(*dims):
        return jax.ShapeDtypeStruct(dims, BF16)

    outs = [shape(128, 4096), shape(16, 4096), shape(16, 768), shape(16, 4096), shape(16, 768)]
    outs += [shape(16, 768), shape(16, 4096)]
    tmp = [shape(4, 4, 4, 2, 8, 4096)] * 3
    tmp += [shape(8, 4, 8, w // 2) for w in WID] * 3
    tmp += [shape(2, 4, 8, 4, 8, w) for w in WID]
    tmp += [shape(2, 4, 8, 8, w // 2) for w in WID]
    tmp += [shape(4, 8, 4, 8, w) for w in WID]
    tmp += [shape(4, 8, 8, w // 2) for w in WID] * 2
    scratch = [pltpu.VMEM((2, 4, 128, w), BF16) for w in WID]
    scratch += [pltpu.VMEM((4, 8, 4, 8, w), BF16) for w in WID]
    scratch += [pltpu.VMEM((4, 8, 8, w // 2), BF16) for w in WID]
    scratch += [pltpu.VMEM((4, 8, 4, 8, w), BF16) for w in WID]
    scratch += [pltpu.VMEM((3, 128, w), BF16) for w in WID]
    scratch += [
        pltpu.VMEM((3, 4, 2, 32, 128), F32),
        pltpu.VMEM((3, 4, 2, 32, 128), F32),
        pltpu.VMEM((3, 12, 256, 128), BF16),
        pltpu.VMEM((3, 4, 256, 1), F32),
        pltpu.VMEM((3, 256, 1), F32),
        pltpu.VMEM((128, 4096), F32),
        pltpu.VMEM((1152, 768), BF16),
        pltpu.VMEM((1152, 768), BF16),
        pltpu.VMEM((128, 4096), BF16),
        pltpu.VMEM((1152, 16), BF16),
        pltpu.VMEM((1152, 32), BF16),
        pltpu.VMEM((16, 4096), F32),
        pltpu.VMEM((16, 768), F32),
        pltpu.VMEM((32, 4096), F32),
        pltpu.VMEM((2, 32, 768), F32),
        pltpu.VMEM((32, 4096), BF16),
        pltpu.VMEM((2, 32, 768), BF16),
        pltpu.SemaphoreType.DMA((99,)),
        pltpu.SemaphoreType.DMA((45,)),
        pltpu.SemaphoreType.DMA((5,)),
    ]
    res = pl.pallas_call(
        block_kernel,
        out_shape=outs + tmp,
        in_specs=[vmem] * 2 + [any_spec] * 7 + [vmem] * 6,
        out_specs=[vmem] * N_OUT + [any_spec] * N_TMP,
        scratch_shapes=scratch,
        compiler_params=pltpu.CompilerParams(
            collective_id=0, has_side_effects=True, vmem_limit_bytes=67043328
        ),
        name="whole_block",
    )(*operands)
    return res[:N_OUT]


def local(rows, grad, choice, weight, wg, wu, wd, ga, go, ua, uo, da, do, gate_pre, up_pre):
    res = whole_block(
        choice.T, weight.T, grad, rows, gate_pre[0], up_pre[0], wg[0], wu[0], wd[0],
        ga[0], go[0], ua[0], uo[0], da[0], do[0],
    )
    return (res[0],) + tuple(v[None] for v in res[1:])


def solution(mesh):
    row = P(("ctx", "ep"), None)
    cube = P(("ctx", "ep"), None, None)
    return jax.shard_map(
        local,
        mesh=mesh,
        in_specs=(row,) * 4 + (cube,) * 11,
        out_specs=(row,) + (cube,) * 6,
        check_vma=False,
    )
```

```python
import jax
import jax.numpy as jnp
from jax import lax
from jax.experimental import pallas as pl
from jax.experimental.pallas import tpu as pltpu
from jax.sharding import PartitionSpec as P

MESH = pl.DeviceIdType.MESH
ROLES = ((0, 1, 2), (1, 2, 0), (2, 0, 1))
WID = (1408, 1408, 1280)
OFF = (0, 1408, 2816)
HALF = ((768, 640), (768, 640), (640, 640))
CHUNK = 256
F32 = jnp.float32
BF16 = jnp.bfloat16
adapter_scale = 2.0


def coords():
    c = lax.axis_index("ctx")
    e = lax.axis_index("ep")
    x = lax.rem(c, 4)
    y = c // 8
    z = (e // 2) * 2 + lax.rem(c // 4, 2)
    return (x, y, z), lax.rem(e, 2)


def device(pos, core):
    x, y, z = pos
    return ((y * 2 + lax.rem(z, 2)) * 4 + x, (z // 2) * 2 + core)


def moved(pos, axis, d):
    out = list(pos)
    out[axis] = lax.rem(pos[axis] + d, 4)
    return tuple(out)


def greet(pos, core):
    barrier = pltpu.get_barrier_semaphore()
    other = 1 - core
    peers = [device(pos, other)]
    for axis in range(3):
        for d in (1, 2, 3):
            peers.append(device(moved(pos, axis, d), core))
            peers.append(device(moved(pos, axis, d), other))
    for peer in peers:
        pl.semaphore_signal(barrier, inc=1, device_id=peer, device_id_type=MESH)
    return barrier, len(peers)


def remote(src, dst, ssem, rsem, dev):
    return pltpu.make_async_remote_copy(
        src_ref=src, dst_ref=dst, send_sem=ssem, recv_sem=rsem, device_id=dev, device_id_type=MESH
    )


def expert_ids(j, shape):
    i = lax.broadcasted_iota(jnp.int32, shape, 0)
    v = [None] * 3
    a, b, c = ROLES[j]
    v[a] = i // 32
    v[b] = (i // 8) % 4
    v[c] = (i // 2) % 4
    k = i % 2
    x, y, z = v
    return ((y * 2 + z % 2) * 4 + x) * 4 + (z // 2) * 2 + k


def main_at(ref, j, b, c, k):
    ra, rb, rc = ROLES[j]
    idx = [None] * 3
    idx[ra] = slice(None)
    idx[rb] = b
    idx[rc] = c
    return ref.at[idx[0], idx[1], idx[2], k, :, pl.ds(OFF[j], WID[j])]


def cols(j):
    return [(s, min(CHUNK, WID[j] - s)) for s in range(0, WID[j], CHUNK)]


def halves(j, s):
    h0, h1 = HALF[j]
    return (s, h0 + s) if s < h1 else (s,)


def rows_of(i):
    out = []
    for j in range(3):
        ra, rb, rc = ROLES[j]
        v = [None] * 3
        v[rc] = i // 64
        v[rb] = (i // 8) % 4
        v[ra] = i % 4
        out.append((((v[0] * 4 + v[1]) * 4 + v[2]) * 2 + (i // 32) % 2, (i // 4) % 2))
    return out


def slot_of(block, r):
    x, y, z, k = block // 32, (block // 8) % 4, (block // 2) % 4, block % 2
    return (((y * 2 + z % 2) * 4 + x) * 4 + (z // 2) * 2 + k) * 9 + r


def mm(a, b, da, db):
    return lax.dot_general(a, b, (((da,), (db,)), ((), ())), preferred_element_type=F32)


def flat(v):
    n = v.shape[-1]
    return v.astype(F32).reshape(-1, n).astype(BF16)


N_IN = 15
N_OUT = 7
N_TMP = 27


def block_kernel(*refs):
    (ids_ref, wt_ref, g_hbm, x_hbm, gate_hbm, up_hbm, wg_hbm, wu_hbm, wd_hbm, ga, go, ua, uo, da, do) = refs[:N_IN]
    out, o_gi, o_go, o_ui, o_uo, o_di, o_do = refs[N_IN : N_IN + N_OUT]
    tmp = refs[N_IN + N_OUT : N_IN + N_OUT + N_TMP]
    gmain, xmain, rmain = tmp[0:3]
    tails = (tmp[3:6], tmp[6:9])
    rtails = tmp[9:12]
    recv2, recv2t = tmp[12:15], tmp[15:18]
    r1, r1t = tmp[18:21], tmp[21:24]
    r2t_hbm = tmp[24:27]
    sc = refs[N_IN + N_OUT + N_TMP :]
    ag, send2, send2t, r2, got = sc[0:3], sc[3:6], sc[6:9], sc[9:12], sc[12:15]
    (tab, tabr, pm, wmain, wtail, own, gg, gu, gtail, dlora, back, acc_do, acc_di, acc_in, acc_o, wide, narrow, tflat, sems, rsems, lsems) = sc[15:]
    mains = (gmain, xmain)
    data = (g_hbm, x_hbm)
    pos, core = coords()
    other = 1 - core
    barrier, count = greet(pos, core)

    row = lax.broadcasted_iota(jnp.int32, (128, 128), 0)
    lane = lax.broadcasted_iota(jnp.int32, (128, 128), 1)
    strict = (row < lane).astype(BF16)
    for j in range(3):
        eid = expert_ids(j, (128, 128))
        hit = jnp.zeros((128, 128), F32)
        wgt = jnp.zeros((128, 128), F32)
        for k in range(8):
            same = eid == ids_ref[k : k + 1, :]
            hit = hit + jnp.where(same, 1.0, 0.0)
            wgt = wgt + jnp.where(same, wt_ref[k : k + 1, :], 0.0)
        rank = jnp.dot(hit.astype(BF16), strict, preferred_element_type=F32)
        code = jnp.where(hit > 0.5, rank, -1.0)
        tab[j, :, 0] = code.reshape(4, 32, 128)
        tab[j, :, 1] = wgt.reshape(4, 32, 128)
    pl.semaphore_wait(barrier, count)

    def sem(i):
        return sems.at[i]

    def n1(p, j):
        return p * 3 + j

    def nt(j):
        return 6 + j

    def n2(p, j, t):
        return 9 + (p * 3 + j) * 2 + t

    def n3(p, j, t):
        return 21 + (p * 3 + j) * 2 + t

    RB = 33

    def settle(dummy, ssem, rsem):
        done = remote(dummy, dummy, ssem, rsem, device(pos, other))
        done.wait_recv()
        done.wait_send()

    def here(src, dst, s):
        return pltpu.make_async_copy(src, dst, s)

    def stage1(p):
        for j in range(3):
            ra = ROLES[j][0]
            me = pos[ra]
            src = data[p].at[:, pl.ds(OFF[j], WID[j])]
            for d in (1, 2, 3):
                dev = device(moved(pos, ra, d), core)
                if p == 0:
                    to = lax.rem(me + d, 4)
                    remote(tab.at[j, to], tabr.at[j, me], sem(nt(j)), sem(RB + nt(j)), dev).start()
                remote(src, ag[j].at[p, me], sem(n1(p, j)), sem(RB + n1(p, j)), dev).start()
            if p == 0:
                here(tab.at[j, me], tabr.at[j, me], sem(2 * RB + nt(j))).start()
            here(src, ag[j].at[p, me], sem(2 * RB + n1(p, j))).start()

    def wait1(p, j):
        if p == 0:
            settle(tabr.at[j, pl.ds(0, 3)], sem(nt(j)), sem(RB + nt(j)))
            here(tab.at[j, 0], tabr.at[j, 0], sem(2 * RB + nt(j))).wait()
        settle(ag[j].at[p, pl.ds(0, 3)], sem(n1(p, j)), sem(RB + n1(p, j)))
        here(ag[j].at[p, 0], ag[j].at[p, 0], sem(2 * RB + n1(p, j))).wait()

    sub3 = lax.broadcasted_iota(jnp.int32, (32, 8, 128), 1).astype(F32)

    def build_masks(j):
        wt_acc = jnp.zeros((32, 8, 1), F32)
        for a in range(4):
            code = jnp.broadcast_to(tabr[j, a, 0].reshape(32, 1, 128), (32, 8, 128))
            wgt = jnp.broadcast_to(tabr[j, a, 1].reshape(32, 1, 128), (32, 8, 128))
            hit = jnp.where(code == sub3, 1.0, 0.0)
            pm[j, a] = hit.reshape(256, 128).astype(BF16)
            wmain[j, a] = jnp.sum(hit * wgt, axis=2, keepdims=True).reshape(256, 1)
            for h in range(2):
                mine = jnp.where((code == 8.0) & (sub3 == float(h * 4 + a)), 1.0, 0.0)
                pm[j, 4 + h * 4 + a] = mine.reshape(256, 128).astype(BF16)
                wt_acc = wt_acc + jnp.sum(mine * wgt, axis=2, keepdims=True)
        wtail[j] = wt_acc.reshape(256, 1)

    def pack(p, j):
        h0, h1 = HALF[j]

        def per_block(a, carry):
            for s, n in cols(j):
                res = jnp.dot(pm[j, a], ag[j][p, a, :, s : s + n], preferred_element_type=F32)
                if p == 0:
                    res = res * wmain[j, a]
                send2[j][:, :, a, :, s : s + n] = res.reshape(4, 8, 8, n).astype(BF16)
            return carry

        lax.fori_loop(0, 4, per_block, 0)

        def tail_cols(s, n):
            res = jnp.zeros((256, 128), F32)
            for h in range(n):
                for a in range(4):
                    src = ag[j][p, a, :, pl.ds(pl.multiple_of(h * h0 + s, 128), 128)]
                    res = res + jnp.dot(pm[j, 4 + h * 4 + a], src, preferred_element_type=F32)
            if p == 0:
                res = res * wtail[j]
            send2t[j][:, :, :, pl.ds(s, 128)] = res.reshape(4, 8, 8, 128).astype(BF16)

        def per_cols(i, carry):
            tail_cols(pl.multiple_of(i * 128, 128), 2)
            return carry

        lax.fori_loop(0, h1 // 128, per_cols, 0)
        for s in range(h1, h0, 128):
            tail_cols(s, 1)

    def stage2(p, j):
        rb = ROLES[j][1]
        me = pos[rb]
        for t, (a, b) in enumerate(((send2, recv2), (send2t, recv2t))):
            for d in (1, 2, 3):
                to = lax.rem(me + d, 4)
                dev = device(moved(pos, rb, d), core)
                remote(a[j].at[to], b[j].at[p, me], sem(n2(p, j, t)), sem(RB + n2(p, j, t)), dev).start()
            here(a[j].at[me], b[j].at[p, me], sem(2 * RB + n2(p, j, t))).start()

    def wait2(p, j):
        for t, ref in ((0, recv2), (1, recv2t)):
            settle(ref[j].at[p, pl.ds(0, 3)], sem(n2(p, j, t)), sem(RB + n2(p, j, t)))
            here(ref[j].at[p, 0], ref[j].at[p, 0], sem(2 * RB + n2(p, j, t))).wait()

    def stage3(p, j):
        ra, rb, rc = ROLES[j]
        for d in (1, 2, 3, 0):
            dst_pos = moved(pos, rc, d)
            for flip in (0, 1):
                k = core if flip == 0 else other
                ck = dst_pos[rc] * 2 + k
                dev = device(dst_pos, k)
                for b in range(4):
                    src = recv2[j].at[p, b, ck]
                    dst = main_at(mains[p], j, b, pos[rc], core)
                    if d == 0 and flip == 0:
                        here(src, dst, sem(2 * RB + n3(p, j, 0))).start()
                    else:
                        remote(src, dst, sem(n3(p, j, 0)), sem(RB + n3(p, j, 0)), dev).start()
                src = recv2t[j].at[p, :, ck]
                dst = tails[p][j].at[pos[rc] * 2 + core]
                if d == 0 and flip == 0:
                    here(src, dst, sem(2 * RB + n3(p, j, 1))).start()
                else:
                    remote(src, dst, sem(n3(p, j, 1)), sem(RB + n3(p, j, 1)), dev).start()

    def wait3(p, j):
        for t, ref in ((0, recv2), (1, recv2t)):
            settle(ref[j].at[p, :, pl.ds(0, 7)], sem(n3(p, j, t)), sem(RB + n3(p, j, t)))
            dummy = ref[j].at[p, :, 0]
            here(dummy, dummy, sem(2 * RB + n3(p, j, t))).wait()

    RR = 15

    def rsem(i):
        return rsems.at[i]

    def m1(j, t):
        return j * 2 + t

    def m2(j, t):
        return 6 + j * 2 + t

    def back1(j):
        ra, rb, rc = ROLES[j]
        mine = pos[rc] * 2 + core
        for d in (1, 2, 3, 0):
            dst_pos = moved(pos, rc, d)
            for flip in (0, 1):
                k = core if flip == 0 else other
                ck = dst_pos[rc] * 2 + k
                dev = device(dst_pos, k)
                local_copy = d == 0 and flip == 0
                for b in range(4):
                    src = main_at(rmain, j, b, dst_pos[rc], k)
                    dst = r1[j].at[b, mine]
                    if local_copy:
                        here(src, dst, rsem(2 * RR + m1(j, 0))).start()
                    else:
                        remote(src, dst, rsem(m1(j, 0)), rsem(RR + m1(j, 0)), dev).start()
                src = rtails[j].at[ck]
                dst = r1t[j].at[:, mine]
                if local_copy:
                    here(src, dst, rsem(2 * RR + m1(j, 1))).start()
                else:
                    remote(src, dst, rsem(m1(j, 1)), rsem(RR + m1(j, 1)), dev).start()

    def back_wait1(j):
        for t, ref in ((0, r1), (1, r1t)):
            settle(ref[j].at[:, pl.ds(0, 7)], rsem(m1(j, t)), rsem(RR + m1(j, t)))
            dummy = ref[j].at[:, 0]
            here(dummy, dummy, rsem(2 * RR + m1(j, t))).wait()

    def back2(j):
        rb = ROLES[j][1]
        me = pos[rb]
        for t, (a, b) in enumerate(((r1, r2), (r1t, r2t_hbm))):
            for d in (1, 2, 3):
                to = lax.rem(me + d, 4)
                dev = device(moved(pos, rb, d), core)
                remote(a[j].at[to], b[j].at[me], rsem(m2(j, t)), rsem(RR + m2(j, t)), dev).start()
            here(a[j].at[me], b[j].at[me], rsem(2 * RR + m2(j, t))).start()

    def back_wait2(j):
        for t, ref in ((0, r2), (1, r2t_hbm)):
            settle(ref[j].at[pl.ds(0, 3)], rsem(m2(j, t)), rsem(RR + m2(j, t)))
            here(ref[j].at[0], ref[j].at[0], rsem(2 * RR + m2(j, t))).wait()

    def fold(j):
        ra = ROLES[j][0]
        h0, h1 = HALF[j]
        cp = here(r2t_hbm[j], send2t[j], lsems.at[0])
        cp.start()
        cp.wait()
        for s in range(0, h0, 128):
            tflat[:, s : s + 128] = flat(send2t[j][:, :, :, s : s + 128])
        for d in range(4):
            a = lax.rem(pos[ra] + d, 4)
            mt = pm[j, a].T
            tails_mt = [pm[j, 4 + h * 4 + a].T for h in range(2)]

            def fold_cols(s, n):
                tail = tflat[:, pl.ds(s, 128)]
                for h in range(n):
                    s0 = pl.multiple_of(h * h0 + s, 128)
                    rows = flat(r2[j][:, :, a, :, pl.ds(s0, 128)])
                    res = mm(mt, rows, 1, 0) + mm(tails_mt[h], tail, 1, 0)
                    if d == 0:
                        own[:, pl.ds(pl.multiple_of(OFF[j] + s0, 128), 128)] = res
                    else:
                        ag[j][1, d - 1, :, pl.ds(s0, 128)] = res.astype(BF16)

            def per_cols(i, carry):
                fold_cols(pl.multiple_of(i * 128, 128), 2)
                return carry

            lax.fori_loop(0, h1 // 128, per_cols, 0)
            for s in range(h1, h0, 128):
                fold_cols(s, 1)

    def back3(j):
        ra = ROLES[j][0]
        for d in (1, 2, 3):
            dev = device(moved(pos, ra, d), core)
            remote(ag[j].at[1, d - 1], got[j].at[d - 1], rsem(12 + j), rsem(RR + 12 + j), dev).start()

    def finish(j):
        settle(got[j], rsem(12 + j), rsem(RR + 12 + j))
        for s, n in cols(j):
            total = own[:, OFF[j] + s : OFF[j] + s + n]
            for d in range(3):
                total = total + got[j][d, :, s : s + n].astype(F32)
            out[:, OFF[j] + s : OFF[j] + s + n] = total.astype(BF16)

    def tail_picks(j, swap):
        shape = (256, 128) if swap else (128, 256)
        i = lax.broadcasted_iota(jnp.int32, shape, 0 if swap else 1)
        n = lax.broadcasted_iota(jnp.int32, shape, 1 if swap else 0)
        block, half = rows_of(i)[j]
        return [jnp.where((block == n) & (half == h), 1.0, 0.0).astype(BF16) for h in range(2)]

    def load_tail(p, dst, stage):
        for j in range(3):
            w = HALF[j][0]
            cp = here(tails[p][j], stage.at[:, :, :, pl.ds(0, w)], lsems.at[0])
            cp.start()
            cp.wait()
            picks = tail_picks(j, False)
            for s in range(0, w, 128):
                rows = flat(stage[:, :, :, s : s + 128])
                for h, o in enumerate(halves(j, s)):
                    o = OFF[j] + o
                    dst[0:128, o : o + 128] = mm(picks[h], rows, 1, 0).astype(BF16)

    wide[0:16] = ga[...]
    wide[16:32] = ua[...]
    narrow[0, 0:16] = go[...]
    narrow[0, 16:32] = jnp.zeros_like(go)
    narrow[1, 0:16] = jnp.zeros_like(uo)
    narrow[1, 16:32] = uo[...]
    for ref in (acc_do, acc_di, acc_in, acc_o):
        ref[...] = jnp.zeros_like(ref)

    stage1(0)
    stage1(1)
    for j in range(3):
        wait1(0, j)
        build_masks(j)
        pack(0, j)
        stage2(0, j)
    for j in range(3):
        wait2(0, j)
        stage3(0, j)

    def first_half(gate_pre, up_pre, wd, slab, gc, stage):
        loads = [
            here(gate_hbm, gate_pre, lsems.at[1]),
            here(up_hbm, up_pre, lsems.at[2]),
            here(wd_hbm, wd, lsems.at[3]),
        ]
        for cp in loads:
            cp.start()
        for j in range(3):
            wait1(1, j)
            pack(1, j)
            stage2(1, j)
        for cp in loads:
            cp.wait()
        for j in range(3):
            wait3(0, j)

        def rows_at(r0, n, order):
            gate = jnp.dot(order, gate_pre[...], preferred_element_type=F32)
            up = jnp.dot(order, up_pre[...], preferred_element_type=F32)
            sig = jax.nn.sigmoid(gate)
            silu = gate * sig
            hidden = (silu * up).astype(BF16)
            g = gc[0:n]
            dlora[pl.ds(r0, n)] = mm(hidden, da[...], 1, 1).astype(BF16)
            gl = mm(g, do[...], 1, 1).astype(BF16)
            acc_di[...] += mm(gl, hidden, 0, 0)
            gh = mm(g, wd[...], 1, 1) + adapter_scale * mm(gl, da[...], 1, 0)
            gate_grad = (gh * up * sig * (1.0 + gate * (1.0 - sig))).astype(BF16)
            up_grad = (gh * silu).astype(BF16)
            gg[pl.ds(r0, n)] = gate_grad
            gu[pl.ds(r0, n)] = up_grad
            both = mm(gate_grad, narrow[0], 1, 1) + mm(up_grad, narrow[1], 1, 1)
            back[pl.ds(r0, n)] = both.astype(BF16)

        def main_rows(c, carry):
            cp = here(gmain.at[c], slab, lsems.at[0])
            cp.start()
            i = lax.broadcasted_iota(jnp.int32, (256, 1152), 0)
            n = lax.broadcasted_iota(jnp.int32, (256, 1152), 1)
            order = jnp.where(slot_of(c * 32 + i // 8, i % 8) == n, 1.0, 0.0).astype(BF16)
            cp.wait()
            for s in range(0, 4096, 512):
                gc[:, s : s + 512] = flat(slab[:, :, :, :, s : s + 512])
            rows_at(pl.multiple_of(c * 256, 256), 256, order)
            return carry

        lax.fori_loop(0, 4, main_rows, 0)
        for j in range(3):
            wait2(1, j)
            stage3(1, j)
        load_tail(0, gtail, stage)
        i = lax.broadcasted_iota(jnp.int32, (128, 1152), 0)
        n = lax.broadcasted_iota(jnp.int32, (128, 1152), 1)
        gc[0:128] = gtail[...]
        rows_at(1024, 128, jnp.where(slot_of(i, 8) == n, 1.0, 0.0).astype(BF16))

    pl.run_scoped(
        first_half,
        pltpu.VMEM((1152, 768), BF16),
        pltpu.VMEM((1152, 768), BF16),
        pltpu.VMEM((768, 4096), BF16),
        pltpu.VMEM((4, 4, 2, 8, 4096), BF16),
        pltpu.VMEM((256, 4096), BF16),
        pltpu.VMEM((8, 4, 8, 768), BF16),
    )

    def second_half(wgu, ro, ro_last, tail_out, tail_pack):
        for j in range(3):
            w = WID[j]
            h0, h1 = HALF[j]
            loads = [
                here(src.at[pl.ds(OFF[j], w)], wgu.at[t, pl.ds(0, w)], lsems.at[1 + t])
                for t, src in enumerate((wg_hbm, wu_hbm))
            ]
            for cp in loads:
                cp.start()
            for cp in loads:
                cp.wait()

            def rows(r0, n, s, width):
                o = pl.multiple_of(OFF[j] + s, 128)
                res = mm(gg[r0 : r0 + n], wgu[0, pl.ds(s, width)], 1, 1)
                res = res + mm(gu[r0 : r0 + n], wgu[1, pl.ds(s, width)], 1, 1)
                return res + adapter_scale * mm(back[r0 : r0 + n], wide[:, pl.ds(o, width)], 1, 0)

            def per_cols(i, carry):
                s = pl.multiple_of(i * CHUNK, CHUNK)
                o = pl.multiple_of(OFF[j] + s, 128)
                slot = lax.rem(i, 2)

                @pl.when(i >= 2)
                def _():
                    here(ro.at[0], rmain.at[:, :, :, :, :, pl.ds(0, CHUNK)], lsems.at[3 + slot]).wait()

                for x in range(4):
                    ro[slot, x] = rows(x * 256, 256, s, CHUNK).reshape(4, 4, 2, 8, CHUNK).astype(BF16)
                tail_out[:, pl.ds(s, CHUNK)] = rows(1024, 128, s, CHUNK).astype(BF16)
                here(ro.at[slot], rmain.at[:, :, :, :, :, pl.ds(o, CHUNK)], lsems.at[3 + slot]).start()
                return carry

            lax.fori_loop(0, w // CHUNK, per_cols, 0)
            s = w // CHUNK * CHUNK
            if s < w:
                last = here(ro_last, rmain.at[:, :, :, :, :, pl.ds(OFF[j] + s, 128)], lsems.at[5])
                for x in range(4):
                    ro_last[x] = rows(x * 256, 256, s, 128).reshape(4, 4, 2, 8, 128).astype(BF16)
                tail_out[:, s:w] = rows(1024, 128, s, 128).astype(BF16)
                last.start()
            picks = tail_picks(j, True)
            for s in range(0, h0, 128):
                res = mm(picks[0], tail_out[:, s : s + 128], 1, 0)
                if s < h1:
                    res = res + mm(picks[1], tail_out[:, h0 + s : h0 + s + 128], 1, 0)
                tail_pack[:, :, :, s : s + 128] = res.reshape(8, 4, 8, 128).astype(BF16)
            cp = here(tail_pack.at[:, :, :, pl.ds(0, h0)], rtails[j], lsems.at[0])
            cp.start()
            for slot in range(2):
                here(ro.at[0], rmain.at[:, :, :, :, :, pl.ds(0, CHUNK)], lsems.at[3 + slot]).wait()
            cp.wait()
            if w % CHUNK:
                last.wait()
            back1(j)

    pl.run_scoped(
        second_half,
        pltpu.VMEM((2, 1408, 768), BF16),
        pltpu.VMEM((2, 4, 4, 4, 2, 8, CHUNK), BF16),
        pltpu.VMEM((4, 4, 4, 2, 8, 128), BF16),
        pltpu.VMEM((128, 1408), BF16),
        pltpu.VMEM((8, 4, 8, 768), BF16),
    )

    for j in range(3):
        wait3(1, j)

    def adapters(slab, xc, gc, stage):
        def add(r0, n, g, x):
            deltas = mm(x, wide[...], 1, 1).astype(BF16)
            acc_o[0] += mm(deltas, gg[pl.ds(r0, n)], 0, 0)
            acc_o[1] += mm(deltas, gu[pl.ds(r0, n)], 0, 0)
            lora = back[pl.ds(r0, n)]
            down = dlora[pl.ds(r0, n)]
            acc_in[...] += mm(lora, x, 0, 0)
            acc_do[...] += mm(down, g, 0, 0)

        def main_rows(c, carry):
            cps = [here(gmain.at[c], slab.at[0], lsems.at[1]), here(xmain.at[c], slab.at[1], lsems.at[2])]
            for cp in cps:
                cp.start()
            for cp in cps:
                cp.wait()
            for s in range(0, 4096, 512):
                gc[:, s : s + 512] = flat(slab[0, :, :, :, :, s : s + 512])
                xc[:, s : s + 512] = flat(slab[1, :, :, :, :, s : s + 512])
            add(pl.multiple_of(c * 256, 256), 256, gc[...], xc[...])
            return carry

        lax.fori_loop(0, 4, main_rows, 0)
        for j in range(3):
            back_wait1(j)
            back2(j)
        load_tail(1, xc, stage)
        add(1024, 128, gtail[...], xc[0:128])

    pl.run_scoped(
        adapters,
        pltpu.VMEM((2, 4, 4, 2, 8, 4096), BF16),
        pltpu.VMEM((256, 4096), BF16),
        pltpu.VMEM((256, 4096), BF16),
        pltpu.VMEM((8, 4, 8, 768), BF16),
    )
    o_gi[...] = (adapter_scale * acc_in[0:16]).astype(BF16)
    o_ui[...] = (adapter_scale * acc_in[16:32]).astype(BF16)
    o_go[...] = (adapter_scale * acc_o[0, 0:16]).astype(BF16)
    o_uo[...] = (adapter_scale * acc_o[1, 16:32]).astype(BF16)
    o_di[...] = (adapter_scale * acc_di[...]).astype(BF16)
    o_do[...] = (adapter_scale * acc_do[...]).astype(BF16)

    for j in range(3):
        back_wait2(j)
        fold(j)
        back3(j)
    for j in range(3):
        finish(j)


def whole_block(*operands):
    any_spec = pl.BlockSpec(memory_space=pl.ANY)
    vmem = pl.BlockSpec(memory_space=pltpu.VMEM)

    def shape(*dims):
        return jax.ShapeDtypeStruct(dims, BF16)

    outs = [shape(128, 4096), shape(16, 4096), shape(16, 768), shape(16, 4096), shape(16, 768)]
    outs += [shape(16, 768), shape(16, 4096)]
    tmp = [shape(4, 4, 4, 2, 8, 4096)] * 3
    tmp += [shape(8, 4, 8, h) for h, _ in HALF] * 3
    tmp += [shape(2, 4, 8, 4, 8, w) for w in WID]
    tmp += [shape(2, 4, 8, 8, h) for h, _ in HALF]
    tmp += [shape(4, 8, 4, 8, w) for w in WID]
    tmp += [shape(4, 8, 8, h) for h, _ in HALF] * 2
    scratch = [pltpu.VMEM((2, 4, 128, w), BF16) for w in WID]
    scratch += [pltpu.VMEM((4, 8, 4, 8, w), BF16) for w in WID]
    scratch += [pltpu.VMEM((4, 8, 8, h), BF16) for h, _ in HALF]
    scratch += [pltpu.VMEM((4, 8, 4, 8, w), BF16) for w in WID]
    scratch += [pltpu.VMEM((3, 128, w), BF16) for w in WID]
    scratch += [
        pltpu.VMEM((3, 4, 2, 32, 128), F32),
        pltpu.VMEM((3, 4, 2, 32, 128), F32),
        pltpu.VMEM((3, 12, 256, 128), BF16),
        pltpu.VMEM((3, 4, 256, 1), F32),
        pltpu.VMEM((3, 256, 1), F32),
        pltpu.VMEM((128, 4096), F32),
        pltpu.VMEM((1152, 768), BF16),
        pltpu.VMEM((1152, 768), BF16),
        pltpu.VMEM((128, 4096), BF16),
        pltpu.VMEM((1152, 16), BF16),
        pltpu.VMEM((1152, 32), BF16),
        pltpu.VMEM((16, 4096), F32),
        pltpu.VMEM((16, 768), F32),
        pltpu.VMEM((32, 4096), F32),
        pltpu.VMEM((2, 32, 768), F32),
        pltpu.VMEM((32, 4096), BF16),
        pltpu.VMEM((2, 32, 768), BF16),
        pltpu.VMEM((256, 768), BF16),
        pltpu.SemaphoreType.DMA((99,)),
        pltpu.SemaphoreType.DMA((45,)),
        pltpu.SemaphoreType.DMA((6,)),
    ]
    res = pl.pallas_call(
        block_kernel,
        out_shape=outs + tmp,
        in_specs=[vmem] * 2 + [any_spec] * 7 + [vmem] * 6,
        out_specs=[vmem] * N_OUT + [any_spec] * N_TMP,
        scratch_shapes=scratch,
        compiler_params=pltpu.CompilerParams(
            collective_id=0, has_side_effects=True, vmem_limit_bytes=67043328
        ),
        name="whole_block",
    )(*operands)
    return res[:N_OUT]


def hand_over_kernel(*refs):
    for src, dst in zip(refs[:N_OUT], refs[N_OUT:]):
        dst[...] = src[...]


def hand_over(arrays):
    vmem = pl.BlockSpec(memory_space=pltpu.VMEM)
    return pl.pallas_call(
        hand_over_kernel,
        out_shape=[jax.ShapeDtypeStruct(a.shape, a.dtype) for a in arrays],
        in_specs=[vmem] * N_OUT,
        out_specs=[vmem] * N_OUT,
        name="hand_over",
    )(*arrays)


def local(rows, grad, choice, weight, wg, wu, wd, ga, go, ua, uo, da, do, gate_pre, up_pre):
    res = whole_block(
        choice.T, weight.T, grad, rows, gate_pre[0], up_pre[0], wg[0], wu[0], wd[0],
        ga[0], go[0], ua[0], uo[0], da[0], do[0],
    )
    res = hand_over(res)
    return (res[0],) + tuple(v[None] for v in res[1:])


def solution(mesh):
    row = P(("ctx", "ep"), None)
    cube = P(("ctx", "ep"), None, None)
    return jax.shard_map(
        local,
        mesh=mesh,
        in_specs=(row,) * 4 + (cube,) * 11,
        out_specs=(row,) + (cube,) * 6,
        check_vma=False,
    )
```

```python
import jax
import jax.numpy as jnp
from jax import lax
from jax.experimental import pallas as pl
from jax.experimental.pallas import tpu as pltpu
from jax.sharding import PartitionSpec as P

MESH = pl.DeviceIdType.MESH
ROLES = ((0, 1, 2), (1, 2, 0), (2, 0, 1))
WID = (1408, 1408, 1280)
OFF = (0, 1408, 2816)
HALF = ((768, 640), (768, 640), (640, 640))
CHUNK = 256
F32 = jnp.float32
BF16 = jnp.bfloat16
adapter_scale = 2.0


def coords():
    c = lax.axis_index("ctx")
    e = lax.axis_index("ep")
    x = lax.rem(c, 4)
    y = c // 8
    z = (e // 2) * 2 + lax.rem(c // 4, 2)
    return (x, y, z), lax.rem(e, 2)


def device(pos, core):
    x, y, z = pos
    return ((y * 2 + lax.rem(z, 2)) * 4 + x, (z // 2) * 2 + core)


def moved(pos, axis, d):
    out = list(pos)
    out[axis] = lax.rem(pos[axis] + d, 4)
    return tuple(out)


def greet(pos, core):
    barrier = pltpu.get_barrier_semaphore()
    other = 1 - core
    peers = [device(pos, other)]
    for axis in range(3):
        for d in (1, 2, 3):
            peers.append(device(moved(pos, axis, d), core))
            peers.append(device(moved(pos, axis, d), other))
    for peer in peers:
        pl.semaphore_signal(barrier, inc=1, device_id=peer, device_id_type=MESH)
    return barrier, len(peers)


def remote(src, dst, ssem, rsem, dev):
    return pltpu.make_async_remote_copy(
        src_ref=src, dst_ref=dst, send_sem=ssem, recv_sem=rsem, device_id=dev, device_id_type=MESH
    )


def expert_ids(j, shape):
    i = lax.broadcasted_iota(jnp.int32, shape, 0)
    v = [None] * 3
    a, b, c = ROLES[j]
    v[a] = i // 32
    v[b] = (i // 8) % 4
    v[c] = (i // 2) % 4
    k = i % 2
    x, y, z = v
    return ((y * 2 + z % 2) * 4 + x) * 4 + (z // 2) * 2 + k


def main_at(ref, j, b, c, k):
    ra, rb, rc = ROLES[j]
    idx = [None] * 3
    idx[ra] = slice(None)
    idx[rb] = b
    idx[rc] = c
    return ref.at[idx[0], idx[1], idx[2], k, :, pl.ds(OFF[j], WID[j])]


def cols(j):
    return [(s, min(CHUNK, WID[j] - s)) for s in range(0, WID[j], CHUNK)]


def halves(j, s):
    h0, h1 = HALF[j]
    return (s, h0 + s) if s < h1 else (s,)


def rows_of(i):
    out = []
    for j in range(3):
        ra, rb, rc = ROLES[j]
        v = [None] * 3
        v[rc] = i // 64
        v[rb] = (i // 8) % 4
        v[ra] = i % 4
        out.append((((v[0] * 4 + v[1]) * 4 + v[2]) * 2 + (i // 32) % 2, (i // 4) % 2))
    return out


def slot_of(block, r):
    x, y, z, k = block // 32, (block // 8) % 4, (block // 2) % 4, block % 2
    return (((y * 2 + z % 2) * 4 + x) * 4 + (z // 2) * 2 + k) * 9 + r


def mm(a, b, da, db):
    return lax.dot_general(a, b, (((da,), (db,)), ((), ())), preferred_element_type=F32)


def flat(v):
    n = v.shape[-1]
    return v.astype(F32).reshape(-1, n).astype(BF16)


N_IN = 15
N_OUT = 7
N_TMP = 27


def block_kernel(*refs):
    (ids_ref, wt_ref, g_hbm, x_hbm, gate_hbm, up_hbm, wg_hbm, wu_hbm, wd_hbm, ga, go, ua, uo, da, do) = refs[:N_IN]
    out, o_gi, o_go, o_ui, o_uo, o_di, o_do = refs[N_IN : N_IN + N_OUT]
    tmp = refs[N_IN + N_OUT : N_IN + N_OUT + N_TMP]
    gmain, xmain, rmain = tmp[0:3]
    tails = (tmp[3:6], tmp[6:9])
    rtails = tmp[9:12]
    recv2, recv2t = tmp[12:15], tmp[15:18]
    r1, r1t = tmp[18:21], tmp[21:24]
    r2t_hbm = tmp[24:27]
    sc = refs[N_IN + N_OUT + N_TMP :]
    ag, send2, send2t, r2, got = sc[0:3], sc[3:6], sc[6:9], sc[9:12], sc[12:15]
    (tab, tabr, pm, wmain, wtail, own, gg, gu, gtail, dlora, back, acc_do, acc_di, acc_in, acc_o, wide, narrow, tflat, sems, rsems, lsems) = sc[15:]
    mains = (gmain, xmain)
    data = (g_hbm, x_hbm)
    pos, core = coords()
    other = 1 - core
    barrier, count = greet(pos, core)

    row = lax.broadcasted_iota(jnp.int32, (128, 128), 0)
    lane = lax.broadcasted_iota(jnp.int32, (128, 128), 1)
    strict = (row < lane).astype(BF16)
    for j in range(3):
        eid = expert_ids(j, (128, 128))
        hit = jnp.zeros((128, 128), F32)
        wgt = jnp.zeros((128, 128), F32)
        for k in range(8):
            same = eid == ids_ref[k : k + 1, :]
            hit = hit + jnp.where(same, 1.0, 0.0)
            wgt = wgt + jnp.where(same, wt_ref[k : k + 1, :], 0.0)
        rank = jnp.dot(hit.astype(BF16), strict, preferred_element_type=F32)
        code = jnp.where(hit > 0.5, rank, -1.0)
        tab[j, :, 0] = code.reshape(4, 32, 128)
        tab[j, :, 1] = wgt.reshape(4, 32, 128)
    pl.semaphore_wait(barrier, count)

    def sem(i):
        return sems.at[i]

    def n1(p, j):
        return p * 3 + j

    def nt(j):
        return 6 + j

    def n2(p, j, t):
        return 9 + (p * 3 + j) * 2 + t

    def n3(p, j, t):
        return 21 + (p * 3 + j) * 2 + t

    RB = 33

    def settle(dummy, ssem, rsem):
        done = remote(dummy, dummy, ssem, rsem, device(pos, other))
        done.wait_recv()
        done.wait_send()

    def here(src, dst, s):
        return pltpu.make_async_copy(src, dst, s)

    def stage1(p):
        for j in range(3):
            ra = ROLES[j][0]
            me = pos[ra]
            src = data[p].at[:, pl.ds(OFF[j], WID[j])]
            for d in (1, 2, 3):
                dev = device(moved(pos, ra, d), core)
                if p == 0:
                    to = lax.rem(me + d, 4)
                    remote(tab.at[j, to], tabr.at[j, me], sem(nt(j)), sem(RB + nt(j)), dev).start()
                remote(src, ag[j].at[p, me], sem(n1(p, j)), sem(RB + n1(p, j)), dev).start()
            if p == 0:
                here(tab.at[j, me], tabr.at[j, me], sem(2 * RB + nt(j))).start()
            here(src, ag[j].at[p, me], sem(2 * RB + n1(p, j))).start()

    def wait1(p, j):
        if p == 0:
            settle(tabr.at[j, pl.ds(0, 3)], sem(nt(j)), sem(RB + nt(j)))
            here(tab.at[j, 0], tabr.at[j, 0], sem(2 * RB + nt(j))).wait()
        settle(ag[j].at[p, pl.ds(0, 3)], sem(n1(p, j)), sem(RB + n1(p, j)))
        here(ag[j].at[p, 0], ag[j].at[p, 0], sem(2 * RB + n1(p, j))).wait()

    sub3 = lax.broadcasted_iota(jnp.int32, (32, 8, 128), 1).astype(F32)

    def build_masks(j):
        wt_acc = jnp.zeros((32, 8, 1), F32)
        for a in range(4):
            code = jnp.broadcast_to(tabr[j, a, 0].reshape(32, 1, 128), (32, 8, 128))
            wgt = jnp.broadcast_to(tabr[j, a, 1].reshape(32, 1, 128), (32, 8, 128))
            hit = jnp.where(code == sub3, 1.0, 0.0)
            pm[j, a] = hit.reshape(256, 128).astype(BF16)
            wmain[j, a] = jnp.sum(hit * wgt, axis=2, keepdims=True).reshape(256, 1)
            for h in range(2):
                mine = jnp.where((code == 8.0) & (sub3 == float(h * 4 + a)), 1.0, 0.0)
                pm[j, 4 + h * 4 + a] = mine.reshape(256, 128).astype(BF16)
                wt_acc = wt_acc + jnp.sum(mine * wgt, axis=2, keepdims=True)
        wtail[j] = wt_acc.reshape(256, 1)

    def pack(p, j):
        h0, h1 = HALF[j]

        def per_block(a, carry):
            for s, n in cols(j):
                res = jnp.dot(pm[j, a], ag[j][p, a, :, s : s + n], preferred_element_type=F32)
                if p == 0:
                    res = res * wmain[j, a]
                send2[j][:, :, a, :, s : s + n] = res.reshape(4, 8, 8, n).astype(BF16)
            return carry

        lax.fori_loop(0, 4, per_block, 0)

        def tail_cols(s, n):
            res = jnp.zeros((256, 128), F32)
            for h in range(n):
                for a in range(4):
                    src = ag[j][p, a, :, pl.ds(pl.multiple_of(h * h0 + s, 128), 128)]
                    res = res + jnp.dot(pm[j, 4 + h * 4 + a], src, preferred_element_type=F32)
            if p == 0:
                res = res * wtail[j]
            send2t[j][:, :, :, pl.ds(s, 128)] = res.reshape(4, 8, 8, 128).astype(BF16)

        def per_cols(i, carry):
            tail_cols(pl.multiple_of(i * 128, 128), 2)
            return carry

        lax.fori_loop(0, h1 // 128, per_cols, 0)
        for s in range(h1, h0, 128):
            tail_cols(s, 1)

    def stage2(p, j):
        rb = ROLES[j][1]
        me = pos[rb]
        for t, (a, b) in enumerate(((send2, recv2), (send2t, recv2t))):
            for d in (1, 2, 3):
                to = lax.rem(me + d, 4)
                dev = device(moved(pos, rb, d), core)
                remote(a[j].at[to], b[j].at[p, me], sem(n2(p, j, t)), sem(RB + n2(p, j, t)), dev).start()
            here(a[j].at[me], b[j].at[p, me], sem(2 * RB + n2(p, j, t))).start()

    def wait2(p, j):
        for t, ref in ((0, recv2), (1, recv2t)):
            settle(ref[j].at[p, pl.ds(0, 3)], sem(n2(p, j, t)), sem(RB + n2(p, j, t)))
            here(ref[j].at[p, 0], ref[j].at[p, 0], sem(2 * RB + n2(p, j, t))).wait()

    def stage3(p, j):
        ra, rb, rc = ROLES[j]
        for d in (1, 2, 3, 0):
            dst_pos = moved(pos, rc, d)
            for flip in (0, 1):
                k = core if flip == 0 else other
                ck = dst_pos[rc] * 2 + k
                dev = device(dst_pos, k)
                for b in range(4):
                    src = recv2[j].at[p, b, ck]
                    dst = main_at(mains[p], j, b, pos[rc], core)
                    if d == 0 and flip == 0:
                        here(src, dst, sem(2 * RB + n3(p, j, 0))).start()
                    else:
                        remote(src, dst, sem(n3(p, j, 0)), sem(RB + n3(p, j, 0)), dev).start()
                src = recv2t[j].at[p, :, ck]
                dst = tails[p][j].at[pos[rc] * 2 + core]
                if d == 0 and flip == 0:
                    here(src, dst, sem(2 * RB + n3(p, j, 1))).start()
                else:
                    remote(src, dst, sem(n3(p, j, 1)), sem(RB + n3(p, j, 1)), dev).start()

    def wait3(p, j):
        for t, ref in ((0, recv2), (1, recv2t)):
            settle(ref[j].at[p, :, pl.ds(0, 7)], sem(n3(p, j, t)), sem(RB + n3(p, j, t)))
            dummy = ref[j].at[p, :, 0]
            here(dummy, dummy, sem(2 * RB + n3(p, j, t))).wait()

    RR = 15

    def rsem(i):
        return rsems.at[i]

    def m1(j, t):
        return j * 2 + t

    def m2(j, t):
        return 6 + j * 2 + t

    def back1(j):
        ra, rb, rc = ROLES[j]
        mine = pos[rc] * 2 + core
        for d in (1, 2, 3, 0):
            dst_pos = moved(pos, rc, d)
            for flip in (0, 1):
                k = core if flip == 0 else other
                ck = dst_pos[rc] * 2 + k
                dev = device(dst_pos, k)
                local_copy = d == 0 and flip == 0
                for b in range(4):
                    src = main_at(rmain, j, b, dst_pos[rc], k)
                    dst = r1[j].at[b, mine]
                    if local_copy:
                        here(src, dst, rsem(2 * RR + m1(j, 0))).start()
                    else:
                        remote(src, dst, rsem(m1(j, 0)), rsem(RR + m1(j, 0)), dev).start()
                src = rtails[j].at[ck]
                dst = r1t[j].at[:, mine]
                if local_copy:
                    here(src, dst, rsem(2 * RR + m1(j, 1))).start()
                else:
                    remote(src, dst, rsem(m1(j, 1)), rsem(RR + m1(j, 1)), dev).start()

    def back_wait1(j):
        for t, ref in ((0, r1), (1, r1t)):
            settle(ref[j].at[:, pl.ds(0, 7)], rsem(m1(j, t)), rsem(RR + m1(j, t)))
            dummy = ref[j].at[:, 0]
            here(dummy, dummy, rsem(2 * RR + m1(j, t))).wait()

    def back2(j):
        rb = ROLES[j][1]
        me = pos[rb]
        for t, (a, b) in enumerate(((r1, r2), (r1t, r2t_hbm))):
            for d in (1, 2, 3):
                to = lax.rem(me + d, 4)
                dev = device(moved(pos, rb, d), core)
                remote(a[j].at[to], b[j].at[me], rsem(m2(j, t)), rsem(RR + m2(j, t)), dev).start()
            here(a[j].at[me], b[j].at[me], rsem(2 * RR + m2(j, t))).start()

    def back_wait2(j):
        for t, ref in ((0, r2), (1, r2t_hbm)):
            settle(ref[j].at[pl.ds(0, 3)], rsem(m2(j, t)), rsem(RR + m2(j, t)))
            here(ref[j].at[0], ref[j].at[0], rsem(2 * RR + m2(j, t))).wait()

    def fold(j):
        ra = ROLES[j][0]
        h0, h1 = HALF[j]
        cp = here(r2t_hbm[j], send2t[j], lsems.at[0])
        cp.start()
        cp.wait()
        for s in range(0, h0, 128):
            tflat[:, s : s + 128] = flat(send2t[j][:, :, :, s : s + 128])
        for d in range(4):
            a = lax.rem(pos[ra] + d, 4)
            mt = pm[j, a].T
            tails_mt = [pm[j, 4 + h * 4 + a].T for h in range(2)]

            def fold_cols(s, n):
                tail = tflat[:, pl.ds(s, 128)]
                for h in range(n):
                    s0 = pl.multiple_of(h * h0 + s, 128)
                    rows = flat(r2[j][:, :, a, :, pl.ds(s0, 128)])
                    res = mm(mt, rows, 1, 0) + mm(tails_mt[h], tail, 1, 0)
                    if d == 0:
                        own[:, pl.ds(pl.multiple_of(OFF[j] + s0, 128), 128)] = res
                    else:
                        ag[j][1, d - 1, :, pl.ds(s0, 128)] = res.astype(BF16)

            def per_cols(i, carry):
                fold_cols(pl.multiple_of(i * 128, 128), 2)
                return carry

            lax.fori_loop(0, h1 // 128, per_cols, 0)
            for s in range(h1, h0, 128):
                fold_cols(s, 1)

    def back3(j):
        ra = ROLES[j][0]
        for d in (1, 2, 3):
            dev = device(moved(pos, ra, d), core)
            remote(ag[j].at[1, d - 1], got[j].at[d - 1], rsem(12 + j), rsem(RR + 12 + j), dev).start()

    def finish(j):
        settle(got[j], rsem(12 + j), rsem(RR + 12 + j))
        for s, n in cols(j):
            total = own[:, OFF[j] + s : OFF[j] + s + n]
            for d in range(3):
                total = total + got[j][d, :, s : s + n].astype(F32)
            out[:, OFF[j] + s : OFF[j] + s + n] = total.astype(BF16)

    def tail_picks(j, swap):
        shape = (256, 128) if swap else (128, 256)
        i = lax.broadcasted_iota(jnp.int32, shape, 0 if swap else 1)
        n = lax.broadcasted_iota(jnp.int32, shape, 1 if swap else 0)
        block, half = rows_of(i)[j]
        return [jnp.where((block == n) & (half == h), 1.0, 0.0).astype(BF16) for h in range(2)]

    def load_tail(p, dst, stage):
        for j in range(3):
            w = HALF[j][0]
            cp = here(tails[p][j], stage.at[:, :, :, pl.ds(0, w)], lsems.at[0])
            cp.start()
            cp.wait()
            picks = tail_picks(j, False)
            for s in range(0, w, 128):
                rows = flat(stage[:, :, :, s : s + 128])
                for h, o in enumerate(halves(j, s)):
                    o = OFF[j] + o
                    dst[0:128, o : o + 128] = mm(picks[h], rows, 1, 0).astype(BF16)

    wide[0:16] = ga[...]
    wide[16:32] = ua[...]
    narrow[0, 0:16] = go[...]
    narrow[0, 16:32] = jnp.zeros_like(go)
    narrow[1, 0:16] = jnp.zeros_like(uo)
    narrow[1, 16:32] = uo[...]
    for ref in (acc_do, acc_di, acc_in, acc_o):
        ref[...] = jnp.zeros_like(ref)

    stage1(0)
    stage1(1)
    for j in range(3):
        wait1(0, j)
        build_masks(j)
        pack(0, j)
        stage2(0, j)
    for j in range(3):
        wait2(0, j)
        stage3(0, j)

    def first_half(gate_pre, up_pre, wd, slab, gc, stage):
        loads = [
            here(gate_hbm, gate_pre, lsems.at[1]),
            here(up_hbm, up_pre, lsems.at[2]),
            here(wd_hbm, wd, lsems.at[3]),
        ]
        for cp in loads:
            cp.start()
        for j in range(3):
            wait1(1, j)
            pack(1, j)
            stage2(1, j)
        for cp in loads:
            cp.wait()

        def sort_rows(r0, n, block, r):
            lane = lax.broadcasted_iota(jnp.int32, (n, 1152), 1)
            order = jnp.where(slot_of(block, r) == lane, 1.0, 0.0).astype(BF16)
            gg[pl.ds(r0, n)] = jnp.dot(order, gate_pre[...], preferred_element_type=F32).astype(BF16)
            gu[pl.ds(r0, n)] = jnp.dot(order, up_pre[...], preferred_element_type=F32).astype(BF16)

        def sort_main(c, carry):
            i = lax.broadcasted_iota(jnp.int32, (256, 1), 0)
            sort_rows(pl.multiple_of(c * 256, 256), 256, c * 32 + i // 8, i % 8)
            return carry

        lax.fori_loop(0, 4, sort_main, 0)
        sort_rows(1024, 128, lax.broadcasted_iota(jnp.int32, (128, 1), 0), 8)
        for j in range(3):
            wait3(0, j)

        def rows_at(r0, n):
            gate = gg[pl.ds(r0, n)].astype(F32)
            up = gu[pl.ds(r0, n)].astype(F32)
            sig = jax.nn.sigmoid(gate)
            silu = gate * sig
            hidden = (silu * up).astype(BF16)
            g = gc[0:n]
            dlora[pl.ds(r0, n)] = mm(hidden, da[...], 1, 1).astype(BF16)
            gl = mm(g, do[...], 1, 1).astype(BF16)
            acc_di[...] += mm(gl, hidden, 0, 0)
            gh = mm(g, wd[...], 1, 1) + adapter_scale * mm(gl, da[...], 1, 0)
            gate_grad = (gh * up * sig * (1.0 + gate * (1.0 - sig))).astype(BF16)
            up_grad = (gh * silu).astype(BF16)
            gg[pl.ds(r0, n)] = gate_grad
            gu[pl.ds(r0, n)] = up_grad
            both = mm(gate_grad, narrow[0], 1, 1) + mm(up_grad, narrow[1], 1, 1)
            back[pl.ds(r0, n)] = both.astype(BF16)

        def main_rows(c, carry):
            here(gmain.at[c], slab, lsems.at[0]).wait()
            for s in range(0, 4096, 512):
                gc[:, s : s + 512] = flat(slab[:, :, :, :, s : s + 512])

            @pl.when(c < 3)
            def _():
                here(gmain.at[c + 1], slab, lsems.at[0]).start()

            rows_at(pl.multiple_of(c * 256, 256), 256)
            return carry

        here(gmain.at[0], slab, lsems.at[0]).start()
        lax.fori_loop(0, 4, main_rows, 0)
        load_tail(0, gtail, stage)
        gc[0:128] = gtail[...]
        rows_at(1024, 128)
        for j in range(3):
            wait2(1, j)
            stage3(1, j)

    pl.run_scoped(
        first_half,
        pltpu.VMEM((1152, 768), BF16),
        pltpu.VMEM((1152, 768), BF16),
        pltpu.VMEM((768, 4096), BF16),
        pltpu.VMEM((4, 4, 2, 8, 4096), BF16),
        pltpu.VMEM((256, 4096), BF16),
        pltpu.VMEM((8, 4, 8, 768), BF16),
    )

    def second_half(wgu, ro, ro_last, tail_out, tail_pack):
        def weights(j):
            w = WID[j]
            return [
                here(src.at[pl.ds(OFF[j], w)], wgu.at[t, pl.ds(0, w)], lsems.at[1 + t])
                for t, src in enumerate((wg_hbm, wu_hbm))
            ]

        for cp in weights(0):
            cp.start()
        for j in range(3):
            w = WID[j]
            h0, h1 = HALF[j]
            for cp in weights(j):
                cp.wait()

            def rows(r0, n, s, width):
                o = pl.multiple_of(OFF[j] + s, 128)
                res = mm(gg[r0 : r0 + n], wgu[0, pl.ds(s, width)], 1, 1)
                res = res + mm(gu[r0 : r0 + n], wgu[1, pl.ds(s, width)], 1, 1)
                return res + adapter_scale * mm(back[r0 : r0 + n], wide[:, pl.ds(o, width)], 1, 0)

            def per_cols(i, carry):
                s = pl.multiple_of(i * CHUNK, CHUNK)
                o = pl.multiple_of(OFF[j] + s, 128)
                slot = lax.rem(i, 2)

                @pl.when(i >= 2)
                def _():
                    here(ro.at[0], rmain.at[:, :, :, :, :, pl.ds(0, CHUNK)], lsems.at[3 + slot]).wait()

                for x in range(4):
                    ro[slot, x] = rows(x * 256, 256, s, CHUNK).reshape(4, 4, 2, 8, CHUNK).astype(BF16)
                tail_out[:, pl.ds(s, CHUNK)] = rows(1024, 128, s, CHUNK).astype(BF16)
                here(ro.at[slot], rmain.at[:, :, :, :, :, pl.ds(o, CHUNK)], lsems.at[3 + slot]).start()
                return carry

            lax.fori_loop(0, w // CHUNK, per_cols, 0)
            s = w // CHUNK * CHUNK
            if s < w:
                last = here(ro_last, rmain.at[:, :, :, :, :, pl.ds(OFF[j] + s, 128)], lsems.at[5])
                for x in range(4):
                    ro_last[x] = rows(x * 256, 256, s, 128).reshape(4, 4, 2, 8, 128).astype(BF16)
                tail_out[:, s:w] = rows(1024, 128, s, 128).astype(BF16)
                last.start()
            if j < 2:
                for cp in weights(j + 1):
                    cp.start()
            picks = tail_picks(j, True)
            for s in range(0, h0, 128):
                res = mm(picks[0], tail_out[:, s : s + 128], 1, 0)
                if s < h1:
                    res = res + mm(picks[1], tail_out[:, h0 + s : h0 + s + 128], 1, 0)
                tail_pack[:, :, :, s : s + 128] = res.reshape(8, 4, 8, 128).astype(BF16)
            cp = here(tail_pack.at[:, :, :, pl.ds(0, h0)], rtails[j], lsems.at[0])
            cp.start()
            for slot in range(2):
                here(ro.at[0], rmain.at[:, :, :, :, :, pl.ds(0, CHUNK)], lsems.at[3 + slot]).wait()
            cp.wait()
            if w % CHUNK:
                last.wait()
            back1(j)

    pl.run_scoped(
        second_half,
        pltpu.VMEM((2, 1408, 768), BF16),
        pltpu.VMEM((2, 4, 4, 4, 2, 8, CHUNK), BF16),
        pltpu.VMEM((4, 4, 4, 2, 8, 128), BF16),
        pltpu.VMEM((128, 1408), BF16),
        pltpu.VMEM((8, 4, 8, 768), BF16),
    )

    for j in range(3):
        wait3(1, j)

    def adapters(slab, xc, gc, stage):
        def add(r0, n, g, x):
            deltas = mm(x, wide[...], 1, 1).astype(BF16)
            acc_o[0] += mm(deltas, gg[pl.ds(r0, n)], 0, 0)
            acc_o[1] += mm(deltas, gu[pl.ds(r0, n)], 0, 0)
            lora = back[pl.ds(r0, n)]
            down = dlora[pl.ds(r0, n)]
            acc_in[...] += mm(lora, x, 0, 0)
            acc_do[...] += mm(down, g, 0, 0)

        def main_rows(c, carry):
            cps = [here(gmain.at[c], slab.at[0], lsems.at[1]), here(xmain.at[c], slab.at[1], lsems.at[2])]
            for cp in cps:
                cp.start()
            for cp in cps:
                cp.wait()
            for s in range(0, 4096, 512):
                gc[:, s : s + 512] = flat(slab[0, :, :, :, :, s : s + 512])
                xc[:, s : s + 512] = flat(slab[1, :, :, :, :, s : s + 512])
            add(pl.multiple_of(c * 256, 256), 256, gc[...], xc[...])
            return carry

        lax.fori_loop(0, 2, main_rows, 0)
        for j in range(3):
            back_wait1(j)
            back2(j)
        lax.fori_loop(2, 4, main_rows, 0)
        load_tail(1, xc, stage)
        add(1024, 128, gtail[...], xc[0:128])

    pl.run_scoped(
        adapters,
        pltpu.VMEM((2, 4, 4, 2, 8, 4096), BF16),
        pltpu.VMEM((256, 4096), BF16),
        pltpu.VMEM((256, 4096), BF16),
        pltpu.VMEM((8, 4, 8, 768), BF16),
    )
    o_gi[...] = (adapter_scale * acc_in[0:16]).astype(BF16)
    o_ui[...] = (adapter_scale * acc_in[16:32]).astype(BF16)
    o_go[...] = (adapter_scale * acc_o[0, 0:16]).astype(BF16)
    o_uo[...] = (adapter_scale * acc_o[1, 16:32]).astype(BF16)
    o_di[...] = (adapter_scale * acc_di[...]).astype(BF16)
    o_do[...] = (adapter_scale * acc_do[...]).astype(BF16)

    for j in range(3):
        back_wait2(j)
        fold(j)
        back3(j)
    for j in range(3):
        finish(j)


def whole_block(*operands):
    any_spec = pl.BlockSpec(memory_space=pl.ANY)
    vmem = pl.BlockSpec(memory_space=pltpu.VMEM)

    def shape(*dims):
        return jax.ShapeDtypeStruct(dims, BF16)

    outs = [shape(128, 4096), shape(16, 4096), shape(16, 768), shape(16, 4096), shape(16, 768)]
    outs += [shape(16, 768), shape(16, 4096)]
    tmp = [shape(4, 4, 4, 2, 8, 4096)] * 3
    tmp += [shape(8, 4, 8, h) for h, _ in HALF] * 3
    tmp += [shape(2, 4, 8, 4, 8, w) for w in WID]
    tmp += [shape(2, 4, 8, 8, h) for h, _ in HALF]
    tmp += [shape(4, 8, 4, 8, w) for w in WID]
    tmp += [shape(4, 8, 8, h) for h, _ in HALF] * 2
    scratch = [pltpu.VMEM((2, 4, 128, w), BF16) for w in WID]
    scratch += [pltpu.VMEM((4, 8, 4, 8, w), BF16) for w in WID]
    scratch += [pltpu.VMEM((4, 8, 8, h), BF16) for h, _ in HALF]
    scratch += [pltpu.VMEM((4, 8, 4, 8, w), BF16) for w in WID]
    scratch += [pltpu.VMEM((3, 128, w), BF16) for w in WID]
    scratch += [
        pltpu.VMEM((3, 4, 2, 32, 128), F32),
        pltpu.VMEM((3, 4, 2, 32, 128), F32),
        pltpu.VMEM((3, 12, 256, 128), BF16),
        pltpu.VMEM((3, 4, 256, 1), F32),
        pltpu.VMEM((3, 256, 1), F32),
        pltpu.VMEM((128, 4096), F32),
        pltpu.VMEM((1152, 768), BF16),
        pltpu.VMEM((1152, 768), BF16),
        pltpu.VMEM((128, 4096), BF16),
        pltpu.VMEM((1152, 16), BF16),
        pltpu.VMEM((1152, 32), BF16),
        pltpu.VMEM((16, 4096), F32),
        pltpu.VMEM((16, 768), F32),
        pltpu.VMEM((32, 4096), F32),
        pltpu.VMEM((2, 32, 768), F32),
        pltpu.VMEM((32, 4096), BF16),
        pltpu.VMEM((2, 32, 768), BF16),
        pltpu.VMEM((256, 768), BF16),
        pltpu.SemaphoreType.DMA((99,)),
        pltpu.SemaphoreType.DMA((45,)),
        pltpu.SemaphoreType.DMA((6,)),
    ]
    res = pl.pallas_call(
        block_kernel,
        out_shape=outs + tmp,
        in_specs=[vmem] * 2 + [any_spec] * 7 + [vmem] * 6,
        out_specs=[vmem] * N_OUT + [any_spec] * N_TMP,
        scratch_shapes=scratch,
        compiler_params=pltpu.CompilerParams(
            collective_id=0, has_side_effects=True, vmem_limit_bytes=67043328
        ),
        name="whole_block",
    )(*operands)
    return res[:N_OUT]


def hand_over_kernel(*refs):
    for src, dst in zip(refs[:N_OUT], refs[N_OUT:]):
        dst[...] = src[...]


def hand_over(arrays):
    vmem = pl.BlockSpec(memory_space=pltpu.VMEM)
    return pl.pallas_call(
        hand_over_kernel,
        out_shape=[jax.ShapeDtypeStruct(a.shape, a.dtype) for a in arrays],
        in_specs=[vmem] * N_OUT,
        out_specs=[vmem] * N_OUT,
        name="hand_over",
    )(*arrays)


def local(rows, grad, choice, weight, wg, wu, wd, ga, go, ua, uo, da, do, gate_pre, up_pre):
    res = whole_block(
        choice.T, weight.T, grad, rows, gate_pre[0], up_pre[0], wg[0], wu[0], wd[0],
        ga[0], go[0], ua[0], uo[0], da[0], do[0],
    )
    res = hand_over(res)
    return (res[0],) + tuple(v[None] for v in res[1:])


def solution(mesh):
    row = P(("ctx", "ep"), None)
    cube = P(("ctx", "ep"), None, None)
    return jax.shard_map(
        local,
        mesh=mesh,
        in_specs=(row,) * 4 + (cube,) * 11,
        out_specs=(row,) + (cube,) * 6,
        check_vma=False,
    )
```
